512 devices in a mesh: ctx: 64 (over z_lo, y, core), tp: 8 (over x, z_hi).
Axes of the slice: x: 4, y: 8, z: 8 (z_hi: 2, z_lo: 4; z = z_hi * 4 + z_lo), core: 2. Of those that a mesh axis runs over, the one named last changes fastest.
Arguments:
- inputs: float32 [16384, 5120], P('ctx', 'tp'), may hold values from -6 to 6
- state_input: float32 [16384, 128], P('ctx'), may hold values from -0.125 to 0.125
- state_output: float32 [16384, 128], P('ctx'), may hold values from -0.125 to 0.125
- decay_codes: int32 [80, 16384], P('tp', 'ctx'), may hold values from 0 to 45000
- output_grad: float32 [16384, 5120], P('ctx', 'tp'), may hold values from -6 to 6
Outputs:
- input_grad: float32 [16384, 5120], P('ctx', 'tp')
- b_grad: float32 [16384, 128], P(('ctx', 'tp'))
- c_grad: float32 [16384, 128], P(('ctx', 'tp'))
- decay_grad: float32 [80, 16384], P('tp', 'ctx')
The draws below stay inside these ranges and needn't reach their ends.
All inputs are finite; a program needn't handle non-finite values.
Results may differ from the reference program's by a relative error of at most 0.00029.
Values sent between devices are 32-bit elements; how exact they have to be, the bound alone decides.
No kernel may reach another device: no remote copies, remote signals or barrier semaphores. Data moves between devices by JAX's collectives and lax.ppermute only.
A program may use at most 64 MiB of HBM per device.

```python
import jax
import jax.numpy as jnp
from jax import lax

HEAD_TOTAL = 80
P_SIZE = 64
N = 128
Q = 256
TOK_DEV = 256
SEQUENCE_TOTAL = 16384


def draw_decay_codes(key, part):
    segment_keys = jax.random.split(key, 11)
    total_length = SEQUENCE_TOTAL
    block_total = total_length // TOK_DEV
    base_cap = 16384 // total_length
    high_code = max(2, 196608 // total_length)
    medium_low = max(1, 737280 // total_length)
    run_total = total_length // 48 + 2
    head_class = jax.random.randint(segment_keys[0], (HEAD_TOTAL, 1), 0, 4)
    multiplier = jax.random.randint(segment_keys[1], (HEAD_TOTAL, block_total, 1), 1, 4)
    multiplier = jnp.broadcast_to(multiplier, (HEAD_TOTAL, block_total, TOK_DEV)).reshape(HEAD_TOTAL, total_length)
    fast_blocks = jax.random.randint(segment_keys[6], (HEAD_TOTAL, block_total, 1), 0, 4)
    fast_blocks = jnp.broadcast_to(fast_blocks, (HEAD_TOTAL, block_total, TOK_DEV)).reshape(HEAD_TOTAL, total_length)
    base_codes = jax.random.randint(segment_keys[2], (HEAD_TOTAL, total_length), 0, 1 << 20) % (multiplier * base_cap + 1)
    run_gaps = jax.random.randint(segment_keys[7], (HEAD_TOTAL, run_total), 40, 153)
    run_lengths = jax.random.randint(segment_keys[8], (HEAD_TOTAL, run_total), 12, 37)
    run_phase = jax.random.randint(segment_keys[9], (HEAD_TOTAL, 1), 0, 96)
    run_ends = jnp.cumsum(run_gaps + run_lengths, axis=1) - run_phase
    run_starts = run_ends - run_lengths
    run_starts = jnp.minimum(jnp.maximum(run_starts, 0), total_length)
    run_ends = jnp.minimum(jnp.maximum(run_ends, 0), total_length)
    head_rows = lax.broadcasted_iota(jnp.int32, (HEAD_TOTAL, run_total), 0)
    run_marks = jnp.zeros((HEAD_TOTAL, total_length + 1), jnp.int32)
    run_marks = run_marks.at[head_rows, run_starts].add(1)
    run_marks = run_marks.at[head_rows, run_ends].add(-1)
    high_here = jnp.cumsum(run_marks, axis=1)[:, :total_length]
    slow_codes = base_codes + high_here * high_code
    medium_codes = jax.random.randint(segment_keys[10], (HEAD_TOTAL, total_length), medium_low, medium_low + medium_low // 9 + 1)
    fast_codes = jax.random.randint(segment_keys[3], (HEAD_TOTAL, total_length), 1300, 2201)
    surge_offsets = jax.random.randint(segment_keys[4], (HEAD_TOTAL, 2), 0, total_length)
    surge_lengths = jax.random.randint(segment_keys[5], (HEAD_TOTAL, 2), 14600, 45001)
    surge_lengths = surge_lengths.at[0, 0].set(45000)
    position_grid = lax.broadcasted_iota(jnp.int32, (HEAD_TOTAL, total_length), 1)
    surge_spans = jnp.max(jnp.where(position_grid[:, :, None] == surge_offsets[:, None, :], surge_lengths[:, None, :], 0), axis=-1)
    fast_here = jnp.logical_and(head_class == 2, fast_blocks == 0)
    uniform_rate = jnp.where(head_class == 3, medium_codes, jnp.where(fast_here, fast_codes, slow_codes))
    return jnp.where(surge_spans > 0, surge_spans, uniform_rate).astype(jnp.int32)


def shard_levels(rng, shape, cuts, low, largest):
    def one(position, parts):
        heights = jax.random.uniform(jax.random.fold_in(jax.random.fold_in(rng, 6), position), (parts,), jnp.float32, low / len(cuts), largest / len(cuts))
        return jnp.repeat(jnp.exp(heights), shape[position] // parts).reshape((-1,) + (1,) * (len(shape) - position - 1))

    level = one(*cuts[0])
    for cut in cuts[1:]:
        level = level * one(*cut)
    return level


def noise(rng, shape, deviation, reach, shards=(), held_as=jnp.bfloat16):
    entries = jax.random.normal(rng, shape, jnp.float32) * deviation
    if len(shards) > 0:
        entries = shard_levels(rng, shape, shards, -0.22, 0.18) * entries
    return jnp.clip(entries, min=-reach, max=reach).astype(held_as)


def setup_inputs(seed: int = 0) -> dict:
    splits = jax.random.split(jax.random.key(seed), 6)
    return {
        "inputs": noise(splits[0], (SEQUENCE_TOTAL, HEAD_TOTAL * P_SIZE), 1.0, 6.0, ((0, 64), (1, 8)), jnp.float32),
        "state_input": noise(splits[1], (SEQUENCE_TOTAL, N), (16 * N) ** -0.5, 0.125, ((0, 64),), jnp.float32),
        "state_output": noise(splits[2], (SEQUENCE_TOTAL, N), (16 * N) ** -0.5, 0.125, ((0, 64),), jnp.float32),
        "decay_codes": draw_decay_codes(jax.random.fold_in(splits[5], 71), 0),
        "output_grad": noise(splits[4], (SEQUENCE_TOTAL, HEAD_TOTAL * P_SIZE), 1.0, 6.0, ((0, 64), (1, 8)), jnp.float32),
    }


PRECISE = lax.Precision.HIGHEST
CODE_UNIT = 2.0 ** (-16)

def decay_parts(log_decay):
    within = jnp.cumsum(log_decay, axis=-1)
    return (within, within[..., -1])

def block_states(values, writers, within, final_log):
    tail_decay = jnp.exp(final_log[..., None] - within)
    return jnp.einsum('hks,hksp,ksn->hkpn', tail_decay, values, writers, precision=PRECISE)

def fold_blocks(start_state, factors, pieces):

    def carry_step(carried_state, element):
        factor, portion = element
        return (factor[:, None, None] * carried_state + portion, carried_state)
    return lax.scan(carry_step, start_state, (jnp.moveaxis(factors, 1, 0), jnp.moveaxis(pieces, 1, 0)))

def ssd_forward(values, writers, readers, log_decay, start_state):
    within, final_log = decay_parts(log_decay)
    row_index = lax.broadcasted_iota(jnp.int32, (Q, Q), 0)
    column_index = lax.broadcasted_iota(jnp.int32, (Q, Q), 1)
    causal = column_index <= row_index
    log_gap = within[..., :, None] - within[..., None, :]
    decay_matrix = jnp.where(causal, jnp.exp(jnp.where(causal, log_gap, 0.0)), 0.0)
    scores = jnp.einsum('ktn,ksn->kts', readers, writers, precision=PRECISE)
    intra_out = jnp.einsum('hkts,hksp->hktp', decay_matrix * scores[None], values, precision=PRECISE)
    pieces = block_states(values, writers, within, final_log)
    end_state, entering = fold_blocks(start_state, jnp.exp(final_log), pieces)
    entering = jnp.moveaxis(entering, 0, 1)
    inter_out = jnp.exp(within)[..., None] * jnp.einsum('ktn,hkpn->hktp', readers, entering, precision=PRECISE)
    return (intra_out + inter_out, end_state)

def reference(inputs, state_input, state_output, decay_codes, output_grad):
    block_count = SEQUENCE_TOTAL // Q
    head_inputs = jnp.transpose(inputs.reshape(SEQUENCE_TOTAL, HEAD_TOTAL, P_SIZE), (1, 0, 2)).reshape(HEAD_TOTAL, 1, block_count, Q, P_SIZE)
    head_grads = jnp.transpose(output_grad.reshape(SEQUENCE_TOTAL, HEAD_TOTAL, P_SIZE), (1, 0, 2)).reshape(HEAD_TOTAL, 1, block_count, Q, P_SIZE)
    log_decay = (-decay_codes.astype(jnp.float32) * CODE_UNIT).reshape(HEAD_TOTAL, 1, block_count, Q)
    writers = state_input.reshape(block_count, Q, N)
    readers = state_output.reshape(block_count, Q, N)
    empty_state = jnp.zeros((1, P_SIZE, N), jnp.float32)

    def one_head(sums, element):
        values, cotangent, decay_row = element

        def forward(values_in, writers_in, readers_in, decay_in):
            return ssd_forward(values_in, writers_in, readers_in, decay_in, empty_state)[0]
        _, pullback = jax.vjp(forward, values, writers, readers, decay_row)
        grad_values, grad_writers, grad_readers, grad_decay = pullback(cotangent)
        return ((sums[0] + grad_writers, sums[1] + grad_readers), (grad_values[0], grad_decay[0]))
    start_sums = (jnp.zeros((block_count, Q, N), jnp.float32), jnp.zeros((block_count, Q, N), jnp.float32))
    (writer_grad, reader_grad), (value_grad, decay_grad) = lax.scan(one_head, start_sums, (head_inputs, head_grads, log_decay))
    input_grad = jnp.transpose(value_grad.reshape(HEAD_TOTAL, SEQUENCE_TOTAL, P_SIZE), (1, 0, 2)).reshape(SEQUENCE_TOTAL, HEAD_TOTAL * P_SIZE)
    return (input_grad, writer_grad.reshape(SEQUENCE_TOTAL, N), reader_grad.reshape(SEQUENCE_TOTAL, N), decay_grad.reshape(HEAD_TOTAL, SEQUENCE_TOTAL))
```

```python
import jax
import jax.numpy as jnp
from jax import lax
from jax.sharding import PartitionSpec as P

Q = 256
PRECISE = lax.Precision.HIGHEST
CODE_UNIT = 2.0 ** (-16)


def swap_cores(value, count):
    return lax.ppermute(value, "ctx", [(i, i ^ 1) for i in range(count)])


def exchange(value, count):
    groups = [[2 * k + c for k in range(count // 2)] for c in range(2)]
    return lax.all_to_all(value, "ctx", 0, 0, axis_index_groups=groups, tiled=True)


def chip_scan(total, chip_decay, is_late, count):
    heads, width, state = total.shape
    chips = count // 2
    per = width // chips
    rows = heads * per
    sliced = jnp.transpose(total.reshape(heads, chips, per, state), (1, 0, 2, 3)).reshape(chips, rows, state)
    decay_row = jnp.pad(chip_decay, (0, state - heads))
    extra = jnp.zeros((chips, 4, state), jnp.float32).at[:, 0, :].set(decay_row)
    got = exchange(jnp.concatenate([sliced, extra], axis=1), count)
    parts = got[:, :rows, :]
    factors = jnp.repeat(got[:, rows, :heads], per, axis=1)[..., None]

    def forward(carry, element):
        factor, part = element
        return factor * carry + part, carry

    parts = jnp.where(is_late, parts, parts[::-1])
    factors = jnp.where(is_late, factors, factors[::-1])
    _, before = lax.scan(forward, jnp.zeros((rows, state), jnp.float32), (factors, parts), unroll=True)
    before = jnp.where(is_late, before, before[::-1])
    back = exchange(before, count)
    return jnp.transpose(back.reshape(chips, heads, per, state), (1, 0, 2, 3)).reshape(heads, width, state)


def dot(spec, a, b):
    return jnp.einsum(spec, a, b, precision=PRECISE)


def per_device(inputs, state_input, state_output, decay_codes, output_grad):
    count = lax.axis_size("ctx")
    heads, rows = decay_codes.shape
    width = inputs.shape[1] // heads
    state = state_input.shape[1]
    is_late = lax.axis_index("ctx") % 2 == 1
    x = inputs
    dy = output_grad
    log_decay = -decay_codes.astype(jnp.float32) * CODE_UNIT
    within = jnp.cumsum(log_decay, axis=1)
    final = within[:, -1]
    head_enter = jnp.exp(within)
    head_tail = jnp.exp(final[:, None] - within)
    enter = jnp.repeat(head_enter.T, width, axis=1)
    tail = jnp.repeat(head_tail.T, width, axis=1)
    decay = jnp.exp(final)
    xs = x * tail
    dys = dy * enter
    ahead = dot("tc,tn->cn", xs, state_input).reshape(heads, width, state)
    pulled = dot("tc,tn->cn", dys, state_output).reshape(heads, width, state)

    sent = jnp.where(is_late, pulled, ahead)
    mine = jnp.where(is_late, ahead, pulled)
    packed = jnp.concatenate(
        [sent.reshape(heads * width, state), jnp.zeros((8, state), jnp.float32).at[0, :heads].set(decay)]
    )
    got = swap_cores(packed, count)
    other = got[: heads * width].reshape(heads, width, state)
    other_decay = got[heads * width, :heads]
    total = mine + decay[:, None, None] * other
    passed = chip_scan(total, decay * other_decay, is_late, count)
    theirs = swap_cores(passed, count)
    through = other_decay[:, None, None] * passed + other
    start = jnp.where(is_late, through, theirs)
    end_grad = jnp.where(is_late, theirs, through)

    row = lax.broadcasted_iota(jnp.int32, (rows, rows), 0)
    column = lax.broadcasted_iota(jnp.int32, (rows, rows), 1)
    causal = column <= row
    gap = within[:, :, None] - within[:, None, :]
    decays = jnp.where(causal, jnp.exp(jnp.where(causal, gap, 0.0)), 0.0)
    scores = dot("tn,sn->ts", state_output, state_input)
    x3 = x.reshape(rows, heads, width)
    dy3 = dy.reshape(rows, heads, width)
    products = dot("thp,shp->hts", dy3, x3)
    mixed = decays * scores[None]
    dx = dot("hts,thp->shp", mixed, dy3).reshape(rows, heads * width)
    pair = mixed * products
    score_grad = jnp.sum(decays * products, axis=0)
    db = dot("ts,tn->sn", score_grad, state_output)
    dc = dot("ts,sn->tn", score_grad, state_input)
    row_part = jnp.sum(pair, axis=2)
    column_part = jnp.sum(pair, axis=1)

    start2 = start.reshape(heads * width, state)
    end2 = end_grad.reshape(heads * width, state)
    dx_far = tail * dot("sn,cn->sc", state_input, end2)
    y_far = dot("tn,cn->tc", state_output, start2)
    db = db + dot("sc,cn->sn", xs, end2)
    dc = dc + dot("tc,cn->tn", dys, start2)
    enter_part = jnp.sum((y_far * dys).reshape(rows, heads, width), axis=2).T
    leave_part = jnp.sum((dx_far * x).reshape(rows, heads, width), axis=2).T
    through_part = decay * jnp.sum(start * end_grad, axis=(1, 2))
    later = (row <= column).astype(jnp.float32)
    earlier = (column < row).astype(jnp.float32)
    decay_grad = (
        dot("ht,ut->hu", row_part - column_part + enter_part, later)
        + dot("hs,us->hu", leave_part, earlier)
        + through_part[:, None]
    )

    both = jnp.stack([db.reshape(-1, rows // lax.axis_size("tp"), state), dc.reshape(-1, rows // lax.axis_size("tp"), state)], axis=1)
    sums = jnp.sum(lax.all_to_all(both, "tp", 0, 0, tiled=True), axis=0)
    return (dx + dx_far, sums[0], sums[1], decay_grad)


def solution(mesh):
    placed = (P("ctx", "tp"), P("ctx", None), P("ctx", None), P("tp", "ctx"), P("ctx", "tp"))
    return jax.shard_map(
        per_device,
        mesh=mesh,
        in_specs=placed,
        out_specs=(P("ctx", "tp"), P(("ctx", "tp"), None), P(("ctx", "tp"), None), P("tp", "ctx")),
        check_vma=False,
    )
```

```python
import functools

import jax
import jax.numpy as jnp
from jax import lax
from jax.experimental import pallas as pl
from jax.experimental.pallas import tpu as pltpu
from jax.sharding import PartitionSpec as P

INTERPRET = False
F32 = jnp.float32
BF16 = jnp.bfloat16
CODE_UNIT = 2.0 ** (-16)
LANES = 128
MASKED = -1e30
GRANT = 12 << 20
LEAD_GRANT = 60 * 1024 * 1024

VMEM = pl.BlockSpec(memory_space=pltpu.VMEM)
SMEM = pl.BlockSpec(memory_space=pltpu.SMEM)
HBM = pl.BlockSpec(memory_space=pltpu.HBM)


def split(a):
    high = a.astype(BF16)
    return high, (a - high.astype(F32)).astype(BF16)


def nn(a, b):
    return lax.dot_general(a, b, (((1,), (0,)), ((), ())), preferred_element_type=F32)


def nt(a, b):
    return lax.dot_general(a, b, (((1,), (1,)), ((), ())), preferred_element_type=F32)


def three(product, a, b):
    return product(a[0], b[0]) + (product(a[0], b[1]) + product(a[1], b[0]))


def iota(shape, axis):
    return lax.broadcasted_iota(jnp.int32, shape, axis)


def spread(columns, pair, rows):
    first = columns[:, 2 * pair : 2 * pair + 1]
    second = columns[:, 2 * pair + 1 : 2 * pair + 2]
    return jnp.where(iota((rows, LANES), 1) < LANES // 2, first, second)


def block_state(scale, source_ref, side_ref, out_ref):
    rows, columns = source_ref.shape
    side = split(side_ref[...])
    for pair in range(columns // LANES):
        part = slice(pair * LANES, (pair + 1) * LANES)
        scaled = source_ref[:, part] * spread(scale, pair, rows)
        out_ref[part, :] = three(nn, split(scaled.T), side)


def halves(codes):
    return (codes >> 8).astype(F32).astype(BF16), (codes & 255).astype(F32).astype(BF16)


def decay_columns(high, low):
    rows = high.shape[1]
    lower = jnp.where(iota((rows, rows), 1) <= iota((rows, rows), 0), 1.0, 0.0).astype(BF16)
    return (256.0 * nt(lower, high) + nt(lower, low)) * -CODE_UNIT


def lead_kernel(
    late_ref, codes_hbm, x_hbm, dy_hbm, b_hbm, c_hbm, sent_ref, pairs_ref,
    codes_ref, source_ref, side_ref, sems,
):
    fetch_codes = pltpu.make_async_copy(codes_hbm, codes_ref, sems.at[0])
    fetch_codes.start()
    fetch_source = pltpu.make_async_copy(x_hbm, source_ref, sems.at[1])
    fetch_side = pltpu.make_async_copy(b_hbm, side_ref, sems.at[2])

    @pl.when(late_ref[0] == 1)
    def _():
        pltpu.make_async_copy(dy_hbm, source_ref, sems.at[1]).start()
        pltpu.make_async_copy(c_hbm, side_ref, sems.at[2]).start()

    @pl.when(late_ref[0] == 0)
    def _():
        fetch_source.start()
        fetch_side.start()

    fetch_codes.wait()
    codes = codes_ref[...]
    heads, rows = codes.shape
    high, low = halves(codes)
    columns = decay_columns(high, low)
    upper = jnp.where(iota((rows, rows), 0) <= iota((rows, rows), 1), 1.0, 0.0).astype(BF16)
    within = (256.0 * nn(high, upper) + nn(low, upper)) * -CODE_UNIT
    pairs_ref[...] = jnp.zeros_like(pairs_ref)
    for pair in range(heads // 2):
        pairs_ref[pair, 0:2, :] = within[2 * pair : 2 * pair + 2, :]
    final = columns[rows - 1 : rows, :]
    decay = jnp.exp(final)
    lane = iota((8, LANES), 1)
    line = jnp.zeros((8, LANES), F32)
    for head in range(heads):
        line = jnp.where(lane == head, decay[:, head : head + 1], line)
    sent_ref[source_ref.shape[1] :, :] = line
    scale = jnp.exp(jnp.where(late_ref[0] == 1, columns, final - columns))
    fetch_side.wait()
    fetch_source.wait()
    block_state(scale, source_ref, side_ref, sent_ref)


def own_kernel(late_ref, codes_ref, x_ref, dy_ref, b_ref, c_ref, own_ref):
    columns = decay_columns(*halves(codes_ref[...]))
    rows = columns.shape[0]

    @pl.when(late_ref[0] == 0)
    def _():
        block_state(jnp.exp(columns), dy_ref, c_ref, own_ref)

    @pl.when(late_ref[0] == 1)
    def _():
        block_state(jnp.exp(columns[rows - 1 : rows, :] - columns), x_ref, b_ref, own_ref)


def chip_kernel(heads, own_ref, sent_ref, got_ref, slab_hbm, total_ref, slab_ref, sems):
    height = own_ref.shape[0]
    width = height // heads
    chips, slab, lanes = slab_ref.shape
    per = height // chips
    mine = sent_ref[height : height + 1, :]
    theirs = got_ref[height : height + 1, :]
    for head in range(heads):
        part = slice(head * width, (head + 1) * width)
        total_ref[part, :] = own_ref[part, :] + mine[:, head : head + 1] * got_ref[part, :]
    both = mine * theirs
    lane = iota((slab - per, lanes), 1)
    line = iota((slab - per, lanes), 0)
    copies = []
    batch = chips // sems.shape[0]
    for chip in range(chips):
        slab_ref[chip, 0:per, :] = total_ref[chip * per : (chip + 1) * per, :]
        extra = jnp.zeros((slab - per, lanes), F32)
        for head in range(heads):
            low = max(head * width - chip * per, 0)
            high = min((head + 1) * width - chip * per, per)
            if low < high:
                here = (lane >= low) & (lane < high) & (line == 0)
                extra = jnp.where(here, both[:, head : head + 1], extra)
        slab_ref[chip, per:slab, :] = extra
        if (chip + 1) % batch == 0:
            part = pl.ds(chip + 1 - batch, batch)
            copies.append(pltpu.make_async_copy(slab_ref.at[part], slab_hbm.at[part], sems.at[len(copies)]))
            copies[-1].start()
    for copy in copies:
        copy.wait()


def scan_kernel(per, late_ref, got_ref, out_ref):
    chips, slab, lanes = got_ref.shape
    diagonal = iota((slab, lanes), 0) == iota((slab, lanes), 1)

    def run(order):
        carried = jnp.zeros((slab, lanes), F32)
        for chip in order:
            factor = jnp.sum(jnp.where(diagonal, got_ref[chip, per : per + 1, :], 0.0), axis=1, keepdims=True)
            for i in range(per // 4):
                out_ref[chip, i] = carried[4 * i : 4 * i + 4, :]
            carried = factor * carried + got_ref[chip]

    @pl.when(late_ref[0] == 1)
    def _():
        run(range(chips))

    @pl.when(late_ref[0] == 0)
    def _():
        run(range(chips - 1, -1, -1))


def unpack(slab_ref, out_ref):
    chips, pieces, tall, _ = slab_ref.shape
    for chip in range(chips):
        for i in range(pieces):
            at = (chip * pieces + i) * tall
            out_ref[at : at + tall, :] = slab_ref[chip, i]


def block_kernel(
    pairs_ref, x_ref, dy_ref, b_ref, c_ref,
    xs_high, xs_low, dys_high, dys_low, dx_ref, pair_ref, db_ref, dc_ref,
    scores_ref, grads_ref,
):
    step = pl.program_id(0)
    rows = x_ref.shape[0]
    half = rows // 2

    @pl.when(step == 0)
    def _():
        scores_ref[...] = three(nt, split(b_ref[...]), split(c_ref[...]))
        grads_ref[...] = jnp.zeros_like(grads_ref)

    lines = pairs_ref[0]
    columns = lines.T
    x = x_ref[...]
    dy = dy_ref[...]
    xs = split(x * spread(jnp.exp(lines.T[rows - 1 : rows, :] - columns), 0, rows))
    dys = split(dy * spread(jnp.exp(columns), 0, rows))
    xs_high[...], xs_low[...] = xs
    dys_high[...], dys_low[...] = dys
    x_high, x_low = split(x)
    left = iota((rows, LANES), 1) < LANES // 2
    lane = iota((rows, LANES), 1)
    sent = jnp.zeros((rows, LANES), F32)
    received = []
    totals = [0.0, 0.0]
    for i in range(2):
        masked = split(jnp.where(left if i == 0 else ~left, dy, 0.0))
        source_sums = []
        target_sum = None
        for b, start in enumerate((0, half)):
            part = slice(start, start + half)
            target = tuple(m[start:, :] for m in masked)
            products = three(nt, (x_high[part], x_low[part]), target)
            gap = lines[i : i + 1, start:] - columns[part, i : i + 1]
            shape = (half, rows - start)
            decays = jnp.exp(jnp.where(iota(shape, 1) >= iota(shape, 0), gap, MASKED))
            scores = scores_ref[part, start:]
            weighted = decays * products
            grads_ref[part, start:] += weighted
            terms = weighted * scores
            source_sums.append(jnp.sum(terms, axis=1, keepdims=True))
            sums = jnp.sum(terms, axis=0, keepdims=True)
            if b == 0:
                target_sum = sums
            else:
                target_sum = jnp.concatenate([target_sum[:, :half], target_sum[:, half:] + sums], axis=1)
            totals[b] += three(nn, split(decays * scores), target)
        sent = jnp.where(lane == i, jnp.concatenate(source_sums, axis=0), sent)
        received.append(target_sum)
    dx_ref[0:half, :] = totals[0]
    dx_ref[half:, :] = totals[1]
    line = iota((8, rows), 0)
    gained = jnp.where(line == 0, received[0], jnp.where(line == 1, received[1], 0.0))
    pair_ref[0] = gained - sent.T[0:8, :]

    @pl.when(step == pl.num_programs(0) - 1)
    def _():
        grads = grads_ref[...]
        db_ref[...] = three(nn, split(grads), split(c_ref[...]))
        dc_ref[...] = three(nn, split(grads.T), split(b_ref[...]))


def through_kernel(
    heads, late_ref, back_ref, got_ref, xs_high, xs_low, dys_high, dys_low, through_hbm, far_ref, through_ref, sem
):
    height = through_ref.shape[0]
    width = height // heads
    unpack(back_ref, through_ref)
    decay = got_ref[height : height + 1, :]
    for head in range(heads):
        part = slice(head * width, (head + 1) * width)
        through_ref[part, :] = decay[:, head : head + 1] * through_ref[part, :] + got_ref[part, :]
    copy = pltpu.make_async_copy(through_ref, through_hbm, sem)
    copy.start()

    @pl.when(late_ref[0] == 1)
    def _():
        far_ref[...] = three(nn, (dys_high[...], dys_low[...]), split(through_ref[...]))

    @pl.when(late_ref[0] == 0)
    def _():
        far_ref[...] = three(nn, (xs_high[...], xs_low[...]), split(through_ref[...]))

    copy.wait()


def rows_kernel(
    late_ref, theirs_ref, xs_high, xs_low, dys_high, dys_low, far_ref, db_ref, dc_ref, out_hbm, state_ref, out_ref, sems
):
    unpack(theirs_ref, state_ref)
    parts, tall, _ = out_ref.shape
    tall = tall // 2

    def send(which, value):
        side = slice(which * tall, (which + 1) * tall)
        for part in range(parts):
            out_ref[part, side, :] = value[part * tall : (part + 1) * tall, :]
        copy = pltpu.make_async_copy(
            out_ref.at[:, pl.ds(which * tall, tall), :], out_hbm.at[:, pl.ds(which * tall, tall), :], sems.at[which]
        )
        copy.start()
        return copy

    @pl.when(late_ref[0] == 1)
    def _():
        first = send(1, dc_ref[...] + far_ref[...])
        second = send(0, db_ref[...] + three(nn, (xs_high[...], xs_low[...]), split(state_ref[...])))
        first.wait()
        second.wait()

    @pl.when(late_ref[0] == 0)
    def _():
        first = send(0, db_ref[...] + far_ref[...])
        second = send(1, dc_ref[...] + three(nn, (dys_high[...], dys_low[...]), split(state_ref[...])))
        first.wait()
        second.wait()


def last_kernel(
    late_ref, pairs_ref, through_ref, slab_ref, x_ref, dy_ref, b_ref, c_ref, near_ref, pair_ref,
    dx_hbm, out_ref, theirs_ref, dx_ref, sems,
):
    rows, height = x_ref.shape
    pairs = height // LANES
    half = LANES // 2
    late = late_ref[0] == 1
    unpack(slab_ref, theirs_ref)
    b, c = split(b_ref[...]), split(c_ref[...])
    picks = jnp.where((iota((8, LANES), 1) < half) == (iota((8, LANES), 0) == 0), 1.0, 0.0)
    picks = jnp.where(iota((8, LANES), 0) < 2, picks, 0.0).astype(BF16)
    first, second = iota((rows, rows), 0), iota((rows, rows), 1)
    earlier = jnp.where(first < second, 1.0, 0.0).astype(BF16)
    line = iota((8, rows), 0)
    copies = []
    left_lines, through_lines, enter_lines = [], [], []
    for pair in range(pairs):
        part = slice(pair * LANES, (pair + 1) * LANES)
        lines = pairs_ref[pair]
        columns = lines.T
        mine, other = through_ref[part, :], theirs_ref[part, :]
        start = jnp.where(late, mine, other)
        end = jnp.where(late, other, mine)
        entered = three(nt, c, split(start)) * spread(jnp.exp(columns), 0, rows)
        leaving = three(nt, b, split(end)) * spread(jnp.exp(columns[rows - 1 : rows, :] - columns), 0, rows)
        dx_ref[:, part] = near_ref[:, part] + leaving
        copies.append(pltpu.make_async_copy(dx_ref.at[:, part], dx_hbm.at[:, part], sems.at[pair]))
        copies[-1].start()
        enter = split(dy_ref[:, part] * entered)
        leave = split(x_ref[:, part] * leaving)
        enter_lines.append(nt(picks, enter[0]) + nt(picks, enter[1]))
        left_lines.append(nt(picks, leave[0]) + nt(picks, leave[1]))
        across = jnp.sum(mine * other, axis=1, keepdims=True)
        passed = [jnp.sum(across[i * half : (i + 1) * half], axis=0, keepdims=True) for i in range(2)]
        decay = jnp.exp(lines[:, rows - 1 : rows])
        through_lines.append(decay * jnp.where(line == 0, passed[0], jnp.where(line == 1, passed[1], 0.0)))
    later = jnp.where(first >= second, 1.0, 0.0).astype(BF16)

    def exact(lines, ones):
        a = jnp.concatenate(lines, axis=0)
        high, low = split(a)
        rest = (a - high.astype(F32) - low.astype(F32)).astype(BF16)
        return nn(high, ones) + (nn(low, ones) + nn(rest, ones))

    gained = exact([pair_ref[p] + enter_lines[p] for p in range(pairs)], later) + exact(left_lines, earlier)
    total = gained + jnp.concatenate(through_lines, axis=0)
    for pair in range(pairs):
        out_ref[2 * pair : 2 * pair + 2, :] = total[8 * pair : 8 * pair + 2, :]
    for copy in copies:
        copy.wait()


def call(kernel, name, in_specs, out_shape, flops, moved, grant=GRANT, **rest):
    return pl.pallas_call(
        kernel,
        name=name,
        in_specs=in_specs,
        out_shape=out_shape,
        cost_estimate=pl.CostEstimate(flops=flops, bytes_accessed=moved, transcendentals=0),
        interpret=INTERPRET,
        compiler_params=pltpu.CompilerParams(vmem_limit_bytes=grant),
        **rest,
    )


def shape(*dims, dtype=F32):
    return jax.ShapeDtypeStruct(dims, dtype)


def stored(*dims):
    return shape(*dims) if INTERPRET else pltpu.HBM(dims, F32)


def swap_cores(value, count):
    return lax.ppermute(value, "ctx", [(i, i ^ 1) for i in range(count)])


def exchange(value, count):
    groups = [[2 * k + c for k in range(count // 2)] for c in range(2)]
    return lax.all_to_all(value, "ctx", 0, 0, axis_index_groups=groups, tiled=True)


def per_device(inputs, state_input, state_output, decay_codes, output_grad):
    count = lax.axis_size("ctx")
    parts = lax.axis_size("tp")
    heads, rows = decay_codes.shape
    height = inputs.shape[1]
    state = state_input.shape[1]
    pairs = height // LANES
    chips = count // 2
    per = height // chips
    slab = -(-(per + 1) // 8) * 8
    late = (lax.axis_index("ctx") & 1).astype(jnp.int32).reshape(1)
    operands = (inputs, output_grad, state_input, state_output)
    wide = rows * height * 4
    square = 2 * rows * height * state * 3

    sent, lines = call(
        lead_kernel, "lead", [SMEM] + [HBM] * 5, (shape(height + 8, state), shape(pairs, 8, rows)),
        square, 2 * wide, out_specs=(VMEM,) * 2, grant=LEAD_GRANT,
        scratch_shapes=[
            pltpu.VMEM((heads, rows), jnp.int32), pltpu.VMEM((rows, height), F32), pltpu.VMEM((rows, state), F32),
            pltpu.SemaphoreType.DMA((3,)),
        ],
    )(late, decay_codes, *operands)
    got = swap_cores(sent, count)
    own = call(
        own_kernel, "own", [SMEM] + [VMEM] * 5, shape(height, state), square, 3 * wide, out_specs=VMEM,
    )(late, decay_codes, *operands)
    total = call(
        functools.partial(chip_kernel, heads), "chip", [VMEM] * 3, stored(chips, slab, state),
        height * state, wide, out_specs=HBM,
        scratch_shapes=[
            pltpu.VMEM((height, state), F32), pltpu.VMEM((chips, slab, state), F32), pltpu.SemaphoreType.DMA((4,)),
        ],
    )(own, sent, got)
    slices = exchange(total, count)

    tile = pl.BlockSpec((rows, LANES), lambda i: (0, i))
    whole = pl.BlockSpec((rows, state), lambda i: (0, 0))
    line = pl.BlockSpec((1, 8, rows), lambda i: (i, 0, 0))
    *scaled, near, pair_sums, db, dc = call(
        block_kernel, "block", [line, tile, tile, whole, whole],
        (*[shape(rows, height, dtype=BF16)] * 4,
         stored(rows, height), stored(pairs, 8, rows), stored(rows, state), stored(rows, state)),
        8 * square, 6 * wide, grid=(pairs,),
        out_specs=[tile] * 5 + [line, whole, whole],
        scratch_shapes=[pltpu.VMEM((rows, rows), F32)] * 2,
    )(lines, *operands)
    slices, *near_parts = lax.optimization_barrier((slices, *scaled, near, pair_sums, db, dc))
    *scaled, near, pair_sums, db, dc = near_parts
    before = call(
        functools.partial(scan_kernel, per), "scan", [SMEM, VMEM], shape(chips, per // 4, 4, state),
        height * state, wide, out_specs=VMEM,
    )(late, slices)
    back = exchange(before, count)
    theirs = swap_cores(back, count)
    through, far = call(
        functools.partial(through_kernel, heads), "through", [SMEM] + [VMEM] * 6,
        (stored(height, state), shape(rows, state)), square, 3 * wide, out_specs=(HBM, VMEM),
        scratch_shapes=[pltpu.VMEM((height, state), F32), pltpu.SemaphoreType.DMA],
    )(late, back, got, *scaled)
    packed = call(
        rows_kernel, "rows", [SMEM] + [VMEM] * 8, stored(parts, 2 * rows // parts, state),
        square, 3 * wide, out_specs=HBM,
        scratch_shapes=[
            pltpu.VMEM((height, state), F32), pltpu.VMEM((parts, 2 * rows // parts, state), F32),
            pltpu.SemaphoreType.DMA((2,)),
        ],
    )(late, theirs, *scaled, far, db, dc)
    summed = jnp.sum(lax.all_to_all(packed, "tp", 0, 0, tiled=True), axis=0)

    input_grad, decay_grad = call(
        last_kernel, "last", [SMEM] + [VMEM] * 9, (shape(rows, height), shape(heads, rows)),
        2 * square, 6 * wide, out_specs=(HBM, VMEM),
        scratch_shapes=[
            pltpu.VMEM((height, state), F32), pltpu.VMEM((rows, height), F32), pltpu.SemaphoreType.DMA((pairs,)),
        ],
    )(late, lines, through, theirs, *operands, near, pair_sums)
    tall = rows // parts
    return (input_grad, summed[:tall], summed[tall:], decay_grad)


def solution(mesh):
    placed = (P("ctx", "tp"), P("ctx", None), P("ctx", None), P("tp", "ctx"), P("ctx", "tp"))
    return jax.shard_map(
        per_device,
        mesh=mesh,
        in_specs=placed,
        out_specs=(P("ctx", "tp"), P(("ctx", "tp"), None), P(("ctx", "tp"), None), P("tp", "ctx")),
        check_vma=False,
    )
```

```python
import functools

import jax
import jax.numpy as jnp
from jax import lax
from jax.experimental import pallas as pl
from jax.experimental.pallas import tpu as pltpu
from jax.sharding import PartitionSpec as P

INTERPRET = False
F32 = jnp.float32
BF16 = jnp.bfloat16
CODE_UNIT = 2.0 ** (-16)
LANES = 128
MASKED = -1e30
GRANT = 12 << 20
LEAD_GRANT = 60 * 1024 * 1024
OUT_FIRST = 20
BACK_FIRST = 20
SUM_FIRST = 3

VMEM = pl.BlockSpec(memory_space=pltpu.VMEM)
SMEM = pl.BlockSpec(memory_space=pltpu.SMEM)
HBM = pl.BlockSpec(memory_space=pltpu.HBM)


def listed(members, first):
    first = first % members
    return [first] + [k for k in range(members) if k != first]


def split(a):
    high = a.astype(BF16)
    return high, (a - high.astype(F32)).astype(BF16)


def nn(a, b):
    return lax.dot_general(a, b, (((1,), (0,)), ((), ())), preferred_element_type=F32)


def nt(a, b):
    return lax.dot_general(a, b, (((1,), (1,)), ((), ())), preferred_element_type=F32)


def three(product, a, b):
    return product(a[0], b[0]) + (product(a[0], b[1]) + product(a[1], b[0]))


def iota(shape, axis):
    return lax.broadcasted_iota(jnp.int32, shape, axis)


def spread(columns, pair, rows):
    first = columns[:, 2 * pair : 2 * pair + 1]
    second = columns[:, 2 * pair + 1 : 2 * pair + 2]
    return jnp.where(iota((rows, LANES), 1) < LANES // 2, first, second)


def block_state(scale, source_ref, side_ref, out_ref):
    rows, columns = source_ref.shape
    side = split(side_ref[...])
    for pair in range(columns // LANES):
        part = slice(pair * LANES, (pair + 1) * LANES)
        scaled = source_ref[:, part] * spread(scale, pair, rows)
        out_ref[part, :] = three(nn, split(scaled.T), side)


def halves(codes):
    return (codes >> 8).astype(F32).astype(BF16), (codes & 255).astype(F32).astype(BF16)


def decay_columns(high, low):
    rows = high.shape[1]
    lower = jnp.where(iota((rows, rows), 1) <= iota((rows, rows), 0), 1.0, 0.0).astype(BF16)
    return (256.0 * nt(lower, high) + nt(lower, low)) * -CODE_UNIT


def lead_kernel(
    late_ref, codes_hbm, x_hbm, dy_hbm, b_hbm, c_hbm, sent_ref, pairs_ref,
    codes_ref, source_ref, side_ref, sems,
):
    fetch_codes = pltpu.make_async_copy(codes_hbm, codes_ref, sems.at[0])
    fetch_codes.start()
    fetch_source = pltpu.make_async_copy(x_hbm, source_ref, sems.at[1])
    fetch_side = pltpu.make_async_copy(b_hbm, side_ref, sems.at[2])

    @pl.when(late_ref[0] == 1)
    def _():
        pltpu.make_async_copy(dy_hbm, source_ref, sems.at[1]).start()
        pltpu.make_async_copy(c_hbm, side_ref, sems.at[2]).start()

    @pl.when(late_ref[0] == 0)
    def _():
        fetch_source.start()
        fetch_side.start()

    fetch_codes.wait()
    codes = codes_ref[...]
    heads, rows = codes.shape
    high, low = halves(codes)
    columns = decay_columns(high, low)
    upper = jnp.where(iota((rows, rows), 0) <= iota((rows, rows), 1), 1.0, 0.0).astype(BF16)
    within = (256.0 * nn(high, upper) + nn(low, upper)) * -CODE_UNIT
    pairs_ref[...] = jnp.zeros_like(pairs_ref)
    for pair in range(heads // 2):
        pairs_ref[pair, 0:2, :] = within[2 * pair : 2 * pair + 2, :]
    final = columns[rows - 1 : rows, :]
    decay = jnp.exp(final)
    lane = iota((8, LANES), 1)
    line = jnp.zeros((8, LANES), F32)
    for head in range(heads):
        line = jnp.where(lane == head, decay[:, head : head + 1], line)
    sent_ref[source_ref.shape[1] :, :] = line
    scale = jnp.exp(jnp.where(late_ref[0] == 1, columns, final - columns))
    fetch_side.wait()
    fetch_source.wait()
    block_state(scale, source_ref, side_ref, sent_ref)


def own_kernel(late_ref, codes_ref, x_ref, dy_ref, b_ref, c_ref, own_ref):
    columns = decay_columns(*halves(codes_ref[...]))
    rows = columns.shape[0]

    @pl.when(late_ref[0] == 0)
    def _():
        block_state(jnp.exp(columns), dy_ref, c_ref, own_ref)

    @pl.when(late_ref[0] == 1)
    def _():
        block_state(jnp.exp(columns[rows - 1 : rows, :] - columns), x_ref, b_ref, own_ref)


def chip_kernel(heads, own_ref, sent_ref, got_ref, slab_hbm, total_ref, slab_ref, sems):
    height = own_ref.shape[0]
    width = height // heads
    chips, slab, lanes = slab_ref.shape
    per = height // chips
    mine = sent_ref[height : height + 1, :]
    theirs = got_ref[height : height + 1, :]
    for head in range(heads):
        part = slice(head * width, (head + 1) * width)
        total_ref[part, :] = own_ref[part, :] + mine[:, head : head + 1] * got_ref[part, :]
    both = mine * theirs
    lane = iota((slab - per, lanes), 1)
    line = iota((slab - per, lanes), 0)
    copies = []
    batch = chips // sems.shape[0]
    for chip in range(chips):
        slab_ref[chip, 0:per, :] = total_ref[chip * per : (chip + 1) * per, :]
        extra = jnp.zeros((slab - per, lanes), F32)
        for head in range(heads):
            low = max(head * width - chip * per, 0)
            high = min((head + 1) * width - chip * per, per)
            if low < high:
                here = (lane >= low) & (lane < high) & (line == 0)
                extra = jnp.where(here, both[:, head : head + 1], extra)
        slab_ref[chip, per:slab, :] = extra
        if (chip + 1) % batch == 0:
            part = pl.ds(chip + 1 - batch, batch)
            copies.append(pltpu.make_async_copy(slab_ref.at[part], slab_hbm.at[part], sems.at[len(copies)]))
            copies[-1].start()
    for copy in copies:
        copy.wait()


def scan_kernel(per, late_ref, got_ref, out_ref):
    chips, slab, lanes = got_ref.shape
    diagonal = iota((slab, lanes), 0) == iota((slab, lanes), 1)

    arrived, leaving = listed(chips, OUT_FIRST), listed(chips, BACK_FIRST)

    def run(order):
        carried = jnp.zeros((slab, lanes), F32)
        for chip in order:
            at, to = arrived.index(chip), leaving.index(chip)
            factor = jnp.sum(jnp.where(diagonal, got_ref[at, per : per + 1, :], 0.0), axis=1, keepdims=True)
            for i in range(per // 4):
                out_ref[to, i] = carried[4 * i : 4 * i + 4, :]
            carried = factor * carried + got_ref[at]

    @pl.when(late_ref[0] == 1)
    def _():
        run(range(chips))

    @pl.when(late_ref[0] == 0)
    def _():
        run(range(chips - 1, -1, -1))


def unpack(slab_ref, out_ref):
    chips, pieces, tall, _ = slab_ref.shape
    owned = listed(chips, OUT_FIRST)
    for place, chip in enumerate(listed(chips, BACK_FIRST)):
        for i in range(pieces):
            at = (owned.index(chip) * pieces + i) * tall
            out_ref[at : at + tall, :] = slab_ref[place, i]


def block_kernel(
    pairs_ref, x_ref, dy_ref, b_ref, c_ref,
    xs_high, xs_low, dys_high, dys_low, dx_ref, pair_ref, db_ref, dc_ref,
    scores_ref, grads_ref,
):
    step = pl.program_id(0)
    rows = x_ref.shape[0]
    half = rows // 2

    @pl.when(step == 0)
    def _():
        scores_ref[...] = three(nt, split(b_ref[...]), split(c_ref[...]))
        grads_ref[...] = jnp.zeros_like(grads_ref)

    lines = pairs_ref[0]
    columns = lines.T
    x = x_ref[...]
    dy = dy_ref[...]
    xs = split(x * spread(jnp.exp(lines.T[rows - 1 : rows, :] - columns), 0, rows))
    dys = split(dy * spread(jnp.exp(columns), 0, rows))
    xs_high[...], xs_low[...] = xs
    dys_high[...], dys_low[...] = dys
    x_high, x_low = split(x)
    left = iota((rows, LANES), 1) < LANES // 2
    lane = iota((rows, LANES), 1)
    sent = jnp.zeros((rows, LANES), F32)
    received = []
    totals = [0.0, 0.0]
    for i in range(2):
        masked = split(jnp.where(left if i == 0 else ~left, dy, 0.0))
        source_sums = []
        target_sum = None
        for b, start in enumerate((0, half)):
            part = slice(start, start + half)
            target = tuple(m[start:, :] for m in masked)
            products = three(nt, (x_high[part], x_low[part]), target)
            gap = lines[i : i + 1, start:] - columns[part, i : i + 1]
            shape = (half, rows - start)
            decays = jnp.exp(jnp.where(iota(shape, 1) >= iota(shape, 0), gap, MASKED))
            scores = scores_ref[part, start:]
            weighted = decays * products
            grads_ref[part, start:] += weighted
            terms = weighted * scores
            source_sums.append(jnp.sum(terms, axis=1, keepdims=True))
            sums = jnp.sum(terms, axis=0, keepdims=True)
            if b == 0:
                target_sum = sums
            else:
                target_sum = jnp.concatenate([target_sum[:, :half], target_sum[:, half:] + sums], axis=1)
            totals[b] += three(nn, split(decays * scores), target)
        sent = jnp.where(lane == i, jnp.concatenate(source_sums, axis=0), sent)
        received.append(target_sum)
    dx_ref[0:half, :] = totals[0]
    dx_ref[half:, :] = totals[1]
    line = iota((8, rows), 0)
    gained = jnp.where(line == 0, received[0], jnp.where(line == 1, received[1], 0.0))
    pair_ref[0] = gained - sent.T[0:8, :]

    @pl.when(step == pl.num_programs(0) - 1)
    def _():
        grads = grads_ref[...]
        db_ref[...] = three(nn, split(grads), split(c_ref[...]))
        dc_ref[...] = three(nn, split(grads.T), split(b_ref[...]))


def through_kernel(
    heads, late_ref, back_ref, got_ref, xs_high, xs_low, dys_high, dys_low, through_hbm, far_ref, through_ref, sem
):
    height = through_ref.shape[0]
    width = height // heads
    unpack(back_ref, through_ref)
    decay = got_ref[height : height + 1, :]
    for head in range(heads):
        part = slice(head * width, (head + 1) * width)
        through_ref[part, :] = decay[:, head : head + 1] * through_ref[part, :] + got_ref[part, :]
    copy = pltpu.make_async_copy(through_ref, through_hbm, sem)
    copy.start()

    @pl.when(late_ref[0] == 1)
    def _():
        far_ref[...] = three(nn, (dys_high[...], dys_low[...]), split(through_ref[...]))

    @pl.when(late_ref[0] == 0)
    def _():
        far_ref[...] = three(nn, (xs_high[...], xs_low[...]), split(through_ref[...]))

    copy.wait()


def rows_kernel(
    late_ref, theirs_ref, xs_high, xs_low, dys_high, dys_low, far_ref, db_ref, dc_ref, out_hbm, state_ref, out_ref, sems
):
    unpack(theirs_ref, state_ref)
    parts, tall, _ = out_ref.shape
    tall = tall // 2
    places = listed(parts, SUM_FIRST)

    def send(which, value):
        side = slice(which * tall, (which + 1) * tall)
        for part in range(parts):
            out_ref[places.index(part), side, :] = value[part * tall : (part + 1) * tall, :]
        copy = pltpu.make_async_copy(
            out_ref.at[:, pl.ds(which * tall, tall), :], out_hbm.at[:, pl.ds(which * tall, tall), :], sems.at[which]
        )
        copy.start()
        return copy

    @pl.when(late_ref[0] == 1)
    def _():
        first = send(1, dc_ref[...] + far_ref[...])
        second = send(0, db_ref[...] + three(nn, (xs_high[...], xs_low[...]), split(state_ref[...])))
        first.wait()
        second.wait()

    @pl.when(late_ref[0] == 0)
    def _():
        first = send(0, db_ref[...] + far_ref[...])
        second = send(1, dc_ref[...] + three(nn, (dys_high[...], dys_low[...]), split(state_ref[...])))
        first.wait()
        second.wait()


def last_kernel(
    late_ref, pairs_ref, through_ref, slab_ref, x_ref, dy_ref, b_ref, c_ref, near_ref, pair_ref,
    dx_hbm, out_ref, theirs_ref, dx_ref, sems,
):
    rows, height = x_ref.shape
    pairs = height // LANES
    half = LANES // 2
    late = late_ref[0] == 1
    unpack(slab_ref, theirs_ref)
    b, c = split(b_ref[...]), split(c_ref[...])
    picks = jnp.where((iota((8, LANES), 1) < half) == (iota((8, LANES), 0) == 0), 1.0, 0.0)
    picks = jnp.where(iota((8, LANES), 0) < 2, picks, 0.0).astype(BF16)
    first, second = iota((rows, rows), 0), iota((rows, rows), 1)
    earlier = jnp.where(first < second, 1.0, 0.0).astype(BF16)
    line = iota((8, rows), 0)
    copies = []
    left_lines, through_lines, enter_lines = [], [], []
    for pair in range(pairs):
        part = slice(pair * LANES, (pair + 1) * LANES)
        lines = pairs_ref[pair]
        columns = lines.T
        mine, other = through_ref[part, :], theirs_ref[part, :]
        start = jnp.where(late, mine, other)
        end = jnp.where(late, other, mine)
        entered = three(nt, c, split(start)) * spread(jnp.exp(columns), 0, rows)
        leaving = three(nt, b, split(end)) * spread(jnp.exp(columns[rows - 1 : rows, :] - columns), 0, rows)
        dx_ref[:, part] = near_ref[:, part] + leaving
        copies.append(pltpu.make_async_copy(dx_ref.at[:, part], dx_hbm.at[:, part], sems.at[pair]))
        copies[-1].start()
        enter = split(dy_ref[:, part] * entered)
        leave = split(x_ref[:, part] * leaving)
        enter_lines.append(nt(picks, enter[0]) + nt(picks, enter[1]))
        left_lines.append(nt(picks, leave[0]) + nt(picks, leave[1]))
        across = jnp.sum(mine * other, axis=1, keepdims=True)
        passed = [jnp.sum(across[i * half : (i + 1) * half], axis=0, keepdims=True) for i in range(2)]
        decay = jnp.exp(lines[:, rows - 1 : rows])
        through_lines.append(decay * jnp.where(line == 0, passed[0], jnp.where(line == 1, passed[1], 0.0)))
    later = jnp.where(first >= second, 1.0, 0.0).astype(BF16)

    def exact(lines, ones):
        a = jnp.concatenate(lines, axis=0)
        high, low = split(a)
        rest = (a - high.astype(F32) - low.astype(F32)).astype(BF16)
        return nn(high, ones) + (nn(low, ones) + nn(rest, ones))

    gained = exact([pair_ref[p] + enter_lines[p] for p in range(pairs)], later) + exact(left_lines, earlier)
    total = gained + jnp.concatenate(through_lines, axis=0)
    for pair in range(pairs):
        out_ref[2 * pair : 2 * pair + 2, :] = total[8 * pair : 8 * pair + 2, :]
    for copy in copies:
        copy.wait()


def call(kernel, name, in_specs, out_shape, flops, moved, grant=GRANT, **rest):
    return pl.pallas_call(
        kernel,
        name=name,
        in_specs=in_specs,
        out_shape=out_shape,
        cost_estimate=pl.CostEstimate(flops=flops, bytes_accessed=moved, transcendentals=0),
        interpret=INTERPRET,
        compiler_params=pltpu.CompilerParams(vmem_limit_bytes=grant),
        **rest,
    )


def shape(*dims, dtype=F32):
    return jax.ShapeDtypeStruct(dims, dtype)


def stored(*dims):
    return shape(*dims) if INTERPRET else pltpu.HBM(dims, F32)


def swap_cores(value, count):
    return lax.ppermute(value, "ctx", [(i, i ^ 1) for i in range(count)])


def exchange(value, count, first):
    groups = [[2 * k + c for k in listed(count // 2, first)] for c in range(2)]
    return lax.all_to_all(value, "ctx", 0, 0, axis_index_groups=groups, tiled=True)


def per_device(inputs, state_input, state_output, decay_codes, output_grad):
    count = lax.axis_size("ctx")
    parts = lax.axis_size("tp")
    heads, rows = decay_codes.shape
    height = inputs.shape[1]
    state = state_input.shape[1]
    pairs = height // LANES
    chips = count // 2
    per = height // chips
    slab = -(-(per + 1) // 8) * 8
    late = (lax.axis_index("ctx") & 1).astype(jnp.int32).reshape(1)
    operands = (inputs, output_grad, state_input, state_output)
    wide = rows * height * 4
    square = 2 * rows * height * state * 3

    sent, lines = call(
        lead_kernel, "lead", [SMEM] + [HBM] * 5, (shape(height + 8, state), shape(pairs, 8, rows)),
        square, 2 * wide, out_specs=(VMEM,) * 2, grant=LEAD_GRANT,
        scratch_shapes=[
            pltpu.VMEM((heads, rows), jnp.int32), pltpu.VMEM((rows, height), F32), pltpu.VMEM((rows, state), F32),
            pltpu.SemaphoreType.DMA((3,)),
        ],
    )(late, decay_codes, *operands)
    got = swap_cores(sent, count)
    own = call(
        own_kernel, "own", [SMEM] + [VMEM] * 5, shape(height, state), square, 3 * wide, out_specs=VMEM,
    )(late, decay_codes, *operands)
    total = call(
        functools.partial(chip_kernel, heads), "chip", [VMEM] * 3, stored(chips, slab, state),
        height * state, wide, out_specs=HBM,
        scratch_shapes=[
            pltpu.VMEM((height, state), F32), pltpu.VMEM((chips, slab, state), F32), pltpu.SemaphoreType.DMA((4,)),
        ],
    )(own, sent, got)
    slices = exchange(total, count, OUT_FIRST)

    tile = pl.BlockSpec((rows, LANES), lambda i: (0, i))
    whole = pl.BlockSpec((rows, state), lambda i: (0, 0))
    line = pl.BlockSpec((1, 8, rows), lambda i: (i, 0, 0))
    *scaled, near, pair_sums, db, dc = call(
        block_kernel, "block", [line, tile, tile, whole, whole],
        (*[shape(rows, height, dtype=BF16)] * 4,
         stored(rows, height), stored(pairs, 8, rows), stored(rows, state), stored(rows, state)),
        8 * square, 6 * wide, grid=(pairs,),
        out_specs=[tile] * 5 + [line, whole, whole],
        scratch_shapes=[pltpu.VMEM((rows, rows), F32)] * 2,
    )(lines, *operands)
    slices, *near_parts = lax.optimization_barrier((slices, *scaled, near, pair_sums, db, dc))
    *scaled, near, pair_sums, db, dc = near_parts
    before = call(
        functools.partial(scan_kernel, per), "scan", [SMEM, VMEM], shape(chips, per // 4, 4, state),
        height * state, wide, out_specs=VMEM,
    )(late, slices)
    back = exchange(before, count, BACK_FIRST)
    theirs = swap_cores(back, count)
    through, far = call(
        functools.partial(through_kernel, heads), "through", [SMEM] + [VMEM] * 6,
        (stored(height, state), shape(rows, state)), square, 3 * wide, out_specs=(HBM, VMEM),
        scratch_shapes=[pltpu.VMEM((height, state), F32), pltpu.SemaphoreType.DMA],
    )(late, back, got, *scaled)
    packed = call(
        rows_kernel, "rows", [SMEM] + [VMEM] * 8, stored(parts, 2 * rows // parts, state),
        square, 3 * wide, out_specs=HBM,
        scratch_shapes=[
            pltpu.VMEM((height, state), F32), pltpu.VMEM((parts, 2 * rows // parts, state), F32),
            pltpu.SemaphoreType.DMA((2,)),
        ],
    )(late, theirs, *scaled, far, db, dc)
    summed = jnp.sum(lax.all_to_all(packed, "tp", 0, 0, axis_index_groups=[listed(parts, SUM_FIRST)], tiled=True), axis=0)

    input_grad, decay_grad = call(
        last_kernel, "last", [SMEM] + [VMEM] * 9, (shape(rows, height), shape(heads, rows)),
        2 * square, 6 * wide, out_specs=(HBM, VMEM),
        scratch_shapes=[
            pltpu.VMEM((height, state), F32), pltpu.VMEM((rows, height), F32), pltpu.SemaphoreType.DMA((pairs,)),
        ],
    )(late, lines, through, theirs, *operands, near, pair_sums)
    tall = rows // parts
    return (input_grad, summed[:tall], summed[tall:], decay_grad)


def solution(mesh):
    placed = (P("ctx", "tp"), P("ctx", None), P("ctx", None), P("tp", "ctx"), P("ctx", "tp"))
    return jax.shard_map(
        per_device,
        mesh=mesh,
        in_specs=placed,
        out_specs=(P("ctx", "tp"), P(("ctx", "tp"), None), P(("ctx", "tp"), None), P("tp", "ctx")),
        check_vma=False,
    )
```

```python
import functools

import jax
import jax.numpy as jnp
from jax import lax
from jax.experimental import pallas as pl
from jax.experimental.pallas import tpu as pltpu
from jax.sharding import PartitionSpec as P

INTERPRET = False
F32 = jnp.float32
BF16 = jnp.bfloat16
CODE_UNIT = 2.0 ** (-16)
LANES = 128
MASKED = -1e30
GRANT = 12 << 20
OUT_FIRST = 20
BACK_FIRST = 20
SUM_FIRST = 3

VMEM = pl.BlockSpec(memory_space=pltpu.VMEM)
SMEM = pl.BlockSpec(memory_space=pltpu.SMEM)
HBM = pl.BlockSpec(memory_space=pltpu.HBM)


def listed(members, first):
    first = first % members
    return [first] + [k for k in range(members) if k != first]


def split(a):
    high = a.astype(BF16)
    return high, (a - high.astype(F32)).astype(BF16)


def nn(a, b):
    return lax.dot_general(a, b, (((1,), (0,)), ((), ())), preferred_element_type=F32)


def nt(a, b):
    return lax.dot_general(a, b, (((1,), (1,)), ((), ())), preferred_element_type=F32)


def three(product, a, b):
    return product(a[0], b[0]) + (product(a[0], b[1]) + product(a[1], b[0]))


def iota(shape, axis):
    return lax.broadcasted_iota(jnp.int32, shape, axis)


def spread(columns, pair, rows):
    first = columns[:, 2 * pair : 2 * pair + 1]
    second = columns[:, 2 * pair + 1 : 2 * pair + 2]
    return jnp.where(iota((rows, LANES), 1) < LANES // 2, first, second)


def pair_state(scale, source_ref, side, pair, out_ref):
    half = LANES // 2
    turned = source_ref[:, pair * LANES : (pair + 1) * LANES].T
    first = turned[:half, :] * scale[2 * pair : 2 * pair + 1, :]
    second = turned[half:, :] * scale[2 * pair + 1 : 2 * pair + 2, :]
    scaled = jnp.concatenate([first, second], axis=0)
    out_ref[pair * LANES : (pair + 1) * LANES, :] = three(nn, split(scaled), side)


def halves(codes):
    return (codes >> 8).astype(F32).astype(BF16), (codes & 255).astype(F32).astype(BF16)


def decay_lines(codes):
    rows = codes.shape[1]
    high, low = halves(codes)
    upper = jnp.where(iota((rows, rows), 0) <= iota((rows, rows), 1), 1.0, 0.0).astype(BF16)
    return (256.0 * nn(high, upper) + nn(low, upper)) * -CODE_UNIT


def lead_kernel(
    late_ref, codes_hbm, x_hbm, dy_hbm, b_hbm, c_hbm,
    sent_ref, pairs_ref, codes_ref, x_ref, dy_ref, b_ref, c_ref, sems,
):
    pairs = x_ref.shape[1] // LANES

    def wide(source, target, slot):
        parts = [pl.ds(pair * LANES, LANES) for pair in range(pairs)]
        return [pltpu.make_async_copy(source.at[:, p], target.at[:, p], sems.at[slot + i]) for i, p in enumerate(parts)]

    fetch_codes = pltpu.make_async_copy(codes_hbm, codes_ref, sems.at[0])
    fetch_codes.start()
    fetch_x = [pltpu.make_async_copy(b_hbm, b_ref, sems.at[1]), *wide(x_hbm, x_ref, 2)]
    fetch_dy = [pltpu.make_async_copy(c_hbm, c_ref, sems.at[2 + pairs]), *wide(dy_hbm, dy_ref, 3 + pairs)]

    @pl.when(late_ref[0] == 1)
    def _():
        for copy in fetch_dy + fetch_x:
            copy.start()

    @pl.when(late_ref[0] == 0)
    def _():
        for copy in fetch_x + fetch_dy:
            copy.start()

    fetch_codes.wait()
    within = decay_lines(codes_ref[...])
    heads, rows = within.shape
    pairs_ref[...] = jnp.zeros_like(pairs_ref)
    for pair in range(pairs):
        pairs_ref[pair, 0:2, :] = within[2 * pair : 2 * pair + 2, :]
    final = within[:, rows - 1 : rows]
    decay = jnp.exp(final)
    lane = iota((8, LANES), 1)
    line = jnp.zeros((8, LANES), F32)
    for head in range(heads):
        line = jnp.where(lane == head, decay[head : head + 1, :], line)
    sent_ref[x_ref.shape[1] :, :] = line

    def run(scale, source_ref, side_ref, copies, others):
        copies[0].wait()
        side = split(side_ref[...])
        for pair in range(pairs):
            copies[1 + pair].wait()
            pair_state(scale, source_ref, side, pair, sent_ref)
        for copy in others:
            copy.wait()

    @pl.when(late_ref[0] == 1)
    def _():
        run(jnp.exp(within), dy_ref, c_ref, fetch_dy, fetch_x)

    @pl.when(late_ref[0] == 0)
    def _():
        run(jnp.exp(final - within), x_ref, b_ref, fetch_x, fetch_dy)


def own_kernel(late_ref, codes_ref, x_ref, dy_ref, b_ref, c_ref, own_ref):
    within = decay_lines(codes_ref[...])
    rows = within.shape[1]

    def run(scale, source_ref, side_ref):
        side = split(side_ref[...])
        for pair in range(source_ref.shape[1] // LANES):
            pair_state(scale, source_ref, side, pair, own_ref)

    @pl.when(late_ref[0] == 0)
    def _():
        run(jnp.exp(within), dy_ref, c_ref)

    @pl.when(late_ref[0] == 1)
    def _():
        run(jnp.exp(within[:, rows - 1 : rows] - within), x_ref, b_ref)


def chip_kernel(heads, own_ref, sent_ref, got_ref, slab_hbm, total_ref, slab_ref, sems):
    height = own_ref.shape[0]
    width = height // heads
    chips, slab, lanes = slab_ref.shape
    per = height // chips
    mine = sent_ref[height : height + 1, :]
    theirs = got_ref[height : height + 1, :]
    for head in range(heads):
        part = slice(head * width, (head + 1) * width)
        total_ref[part, :] = own_ref[part, :] + mine[:, head : head + 1] * got_ref[part, :]
    both = mine * theirs
    lane = iota((slab - per, lanes), 1)
    line = iota((slab - per, lanes), 0)
    copies = []
    batch = chips // sems.shape[0]
    for chip in range(chips):
        slab_ref[chip, 0:per, :] = total_ref[chip * per : (chip + 1) * per, :]
        extra = jnp.zeros((slab - per, lanes), F32)
        for head in range(heads):
            low = max(head * width - chip * per, 0)
            high = min((head + 1) * width - chip * per, per)
            if low < high:
                here = (lane >= low) & (lane < high) & (line == 0)
                extra = jnp.where(here, both[:, head : head + 1], extra)
        slab_ref[chip, per:slab, :] = extra
        if (chip + 1) % batch == 0:
            part = pl.ds(chip + 1 - batch, batch)
            copies.append(pltpu.make_async_copy(slab_ref.at[part], slab_hbm.at[part], sems.at[len(copies)]))
            copies[-1].start()
    for copy in copies:
        copy.wait()


def scan_kernel(per, late_ref, got_ref, out_ref):
    chips, slab, lanes = got_ref.shape
    diagonal = iota((slab, lanes), 0) == iota((slab, lanes), 1)

    arrived, leaving = listed(chips, OUT_FIRST), listed(chips, BACK_FIRST)

    def run(order):
        carried = jnp.zeros((slab, lanes), F32)
        for chip in order:
            at, to = arrived.index(chip), leaving.index(chip)
            factor = jnp.sum(jnp.where(diagonal, got_ref[at, per : per + 1, :], 0.0), axis=1, keepdims=True)
            for i in range(per // 4):
                out_ref[to, i] = carried[4 * i : 4 * i + 4, :]
            carried = factor * carried + got_ref[at]

    @pl.when(late_ref[0] == 1)
    def _():
        run(range(chips))

    @pl.when(late_ref[0] == 0)
    def _():
        run(range(chips - 1, -1, -1))


def unpack(slab_ref, out_ref):
    chips, pieces, tall, _ = slab_ref.shape
    owned = listed(chips, OUT_FIRST)
    for place, chip in enumerate(listed(chips, BACK_FIRST)):
        for i in range(pieces):
            at = (owned.index(chip) * pieces + i) * tall
            out_ref[at : at + tall, :] = slab_ref[place, i]


def block_kernel(
    pairs_ref, x_ref, dy_ref, b_ref, c_ref,
    xs_high, xs_low, dys_high, dys_low, dx_ref, pair_ref, db_ref, dc_ref,
    scores_ref, grads_ref,
):
    step = pl.program_id(0)
    rows = x_ref.shape[0]
    half = rows // 2

    @pl.when(step == 0)
    def _():
        scores_ref[...] = three(nt, split(b_ref[...]), split(c_ref[...]))
        grads_ref[...] = jnp.zeros_like(grads_ref)

    lines = pairs_ref[0]
    columns = lines.T
    x = x_ref[...]
    dy = dy_ref[...]
    xs = split(x * spread(jnp.exp(lines.T[rows - 1 : rows, :] - columns), 0, rows))
    dys = split(dy * spread(jnp.exp(columns), 0, rows))
    xs_high[...], xs_low[...] = xs
    dys_high[...], dys_low[...] = dys
    x_high, x_low = split(x)
    left = iota((rows, LANES), 1) < LANES // 2
    lane = iota((rows, LANES), 1)
    sent = jnp.zeros((rows, LANES), F32)
    received = []
    totals = [0.0, 0.0]
    for i in range(2):
        masked = split(jnp.where(left if i == 0 else ~left, dy, 0.0))
        source_sums = []
        target_sum = None
        for b, start in enumerate((0, half)):
            part = slice(start, start + half)
            target = tuple(m[start:, :] for m in masked)
            products = three(nt, (x_high[part], x_low[part]), target)
            gap = lines[i : i + 1, start:] - columns[part, i : i + 1]
            shape = (half, rows - start)
            decays = jnp.exp(jnp.where(iota(shape, 1) >= iota(shape, 0), gap, MASKED))
            scores = scores_ref[part, start:]
            weighted = decays * products
            grads_ref[part, start:] += weighted
            terms = weighted * scores
            source_sums.append(jnp.sum(terms, axis=1, keepdims=True))
            sums = jnp.sum(terms, axis=0, keepdims=True)
            if b == 0:
                target_sum = sums
            else:
                target_sum = jnp.concatenate([target_sum[:, :half], target_sum[:, half:] + sums], axis=1)
            totals[b] += three(nn, split(decays * scores), target)
        sent = jnp.where(lane == i, jnp.concatenate(source_sums, axis=0), sent)
        received.append(target_sum)
    dx_ref[0:half, :] = totals[0]
    dx_ref[half:, :] = totals[1]
    line = iota((8, rows), 0)
    gained = jnp.where(line == 0, received[0], jnp.where(line == 1, received[1], 0.0))
    pair_ref[0] = gained - sent.T[0:8, :]

    @pl.when(step == pl.num_programs(0) - 1)
    def _():
        grads = grads_ref[...]
        db_ref[...] = three(nn, split(grads), split(c_ref[...]))
        dc_ref[...] = three(nn, split(grads.T), split(b_ref[...]))


def through_kernel(
    heads, late_ref, back_ref, got_ref, xs_high, xs_low, dys_high, dys_low, through_hbm, far_ref, through_ref, sem
):
    height = through_ref.shape[0]
    width = height // heads
    unpack(back_ref, through_ref)
    decay = got_ref[height : height + 1, :]
    for head in range(heads):
        part = slice(head * width, (head + 1) * width)
        through_ref[part, :] = decay[:, head : head + 1] * through_ref[part, :] + got_ref[part, :]
    copy = pltpu.make_async_copy(through_ref, through_hbm, sem)
    copy.start()

    @pl.when(late_ref[0] == 1)
    def _():
        far_ref[...] = three(nn, (dys_high[...], dys_low[...]), split(through_ref[...]))

    @pl.when(late_ref[0] == 0)
    def _():
        far_ref[...] = three(nn, (xs_high[...], xs_low[...]), split(through_ref[...]))

    copy.wait()


def rows_kernel(
    late_ref, theirs_ref, xs_high, xs_low, dys_high, dys_low, far_ref, db_ref, dc_ref, out_hbm, state_ref, out_ref, sems
):
    unpack(theirs_ref, state_ref)
    parts, tall, _ = out_ref.shape
    tall = tall // 2
    places = listed(parts, SUM_FIRST)

    def send(which, value):
        side = slice(which * tall, (which + 1) * tall)
        for part in range(parts):
            out_ref[places.index(part), side, :] = value[part * tall : (part + 1) * tall, :]
        copy = pltpu.make_async_copy(
            out_ref.at[:, pl.ds(which * tall, tall), :], out_hbm.at[:, pl.ds(which * tall, tall), :], sems.at[which]
        )
        copy.start()
        return copy

    @pl.when(late_ref[0] == 1)
    def _():
        first = send(1, dc_ref[...] + far_ref[...])
        second = send(0, db_ref[...] + three(nn, (xs_high[...], xs_low[...]), split(state_ref[...])))
        first.wait()
        second.wait()

    @pl.when(late_ref[0] == 0)
    def _():
        first = send(0, db_ref[...] + far_ref[...])
        second = send(1, dc_ref[...] + three(nn, (dys_high[...], dys_low[...]), split(state_ref[...])))
        first.wait()
        second.wait()


def last_kernel(
    late_ref, pairs_ref, through_ref, slab_ref, x_ref, dy_ref, b_ref, c_ref, near_ref, pair_ref,
    dx_hbm, out_ref, theirs_ref, dx_ref, sems,
):
    rows, height = x_ref.shape
    pairs = height // LANES
    half = LANES // 2
    late = late_ref[0] == 1
    unpack(slab_ref, theirs_ref)
    b, c = split(b_ref[...]), split(c_ref[...])
    picks = jnp.where((iota((8, LANES), 1) < half) == (iota((8, LANES), 0) == 0), 1.0, 0.0)
    picks = jnp.where(iota((8, LANES), 0) < 2, picks, 0.0).astype(BF16)
    first, second = iota((rows, rows), 0), iota((rows, rows), 1)
    earlier = jnp.where(first < second, 1.0, 0.0).astype(BF16)
    line = iota((8, rows), 0)
    copies = []
    left_lines, through_lines, enter_lines = [], [], []
    for pair in range(pairs):
        part = slice(pair * LANES, (pair + 1) * LANES)
        lines = pairs_ref[pair]
        columns = lines.T
        mine, other = through_ref[part, :], theirs_ref[part, :]
        start = jnp.where(late, mine, other)
        end = jnp.where(late, other, mine)
        entered = three(nt, c, split(start)) * spread(jnp.exp(columns), 0, rows)
        leaving = three(nt, b, split(end)) * spread(jnp.exp(columns[rows - 1 : rows, :] - columns), 0, rows)
        dx_ref[:, part] = near_ref[:, part] + leaving
        copies.append(pltpu.make_async_copy(dx_ref.at[:, part], dx_hbm.at[:, part], sems.at[pair]))
        copies[-1].start()
        enter = split(dy_ref[:, part] * entered)
        leave = split(x_ref[:, part] * leaving)
        enter_lines.append(nt(picks, enter[0]) + nt(picks, enter[1]))
        left_lines.append(nt(picks, leave[0]) + nt(picks, leave[1]))
        across = jnp.sum(mine * other, axis=1, keepdims=True)
        passed = [jnp.sum(across[i * half : (i + 1) * half], axis=0, keepdims=True) for i in range(2)]
        decay = jnp.exp(lines[:, rows - 1 : rows])
        through_lines.append(decay * jnp.where(line == 0, passed[0], jnp.where(line == 1, passed[1], 0.0)))
    later = jnp.where(first >= second, 1.0, 0.0).astype(BF16)

    def exact(lines, ones):
        a = jnp.concatenate(lines, axis=0)
        high, low = split(a)
        rest = (a - high.astype(F32) - low.astype(F32)).astype(BF16)
        return nn(high, ones) + (nn(low, ones) + nn(rest, ones))

    gained = exact([pair_ref[p] + enter_lines[p] for p in range(pairs)], later) + exact(left_lines, earlier)
    total = gained + jnp.concatenate(through_lines, axis=0)
    for pair in range(pairs):
        out_ref[2 * pair : 2 * pair + 2, :] = total[8 * pair : 8 * pair + 2, :]
    for copy in copies:
        copy.wait()


def call(kernel, name, in_specs, out_shape, flops, moved, grant=GRANT, **rest):
    return pl.pallas_call(
        kernel,
        name=name,
        in_specs=in_specs,
        out_shape=out_shape,
        cost_estimate=pl.CostEstimate(flops=flops, bytes_accessed=moved, transcendentals=0),
        interpret=INTERPRET,
        compiler_params=pltpu.CompilerParams(vmem_limit_bytes=grant),
        **rest,
    )


def shape(*dims, dtype=F32):
    return jax.ShapeDtypeStruct(dims, dtype)


def stored(*dims):
    return shape(*dims) if INTERPRET else pltpu.HBM(dims, F32)


def swap_cores(value, count):
    return lax.ppermute(value, "ctx", [(i, i ^ 1) for i in range(count)])


def exchange(value, count, first):
    groups = [[2 * k + c for k in listed(count // 2, first)] for c in range(2)]
    return lax.all_to_all(value, "ctx", 0, 0, axis_index_groups=groups, tiled=True)


def per_device(inputs, state_input, state_output, decay_codes, output_grad):
    count = lax.axis_size("ctx")
    parts = lax.axis_size("tp")
    heads, rows = decay_codes.shape
    height = inputs.shape[1]
    state = state_input.shape[1]
    pairs = height // LANES
    chips = count // 2
    per = height // chips
    slab = -(-(per + 1) // 8) * 8
    late = (lax.axis_index("ctx") & 1).astype(jnp.int32).reshape(1)
    operands = (inputs, output_grad, state_input, state_output)
    wide = rows * height * 4
    square = 2 * rows * height * state * 3

    given = (decay_codes, *operands)
    sent, lines, codes, *operands = call(
        lead_kernel, "lead", [SMEM] + [HBM] * 5,
        (shape(height + 8, state), shape(pairs, 8, rows), *[shape(*a.shape, dtype=a.dtype) for a in given]),
        square, 2 * wide, out_specs=(VMEM,) * 7, scratch_shapes=[pltpu.SemaphoreType.DMA((3 + 2 * pairs,))],
    )(late, *[a if INTERPRET else pltpu.with_memory_space_constraint(a, pltpu.HBM) for a in given])
    got = swap_cores(sent, count)
    own = call(
        own_kernel, "own", [SMEM] + [VMEM] * 5, shape(height, state), square, 3 * wide, out_specs=VMEM,
    )(late, codes, *operands)
    total = call(
        functools.partial(chip_kernel, heads), "chip", [VMEM] * 3, stored(chips, slab, state),
        height * state, wide, out_specs=HBM,
        scratch_shapes=[
            pltpu.VMEM((height, state), F32), pltpu.VMEM((chips, slab, state), F32), pltpu.SemaphoreType.DMA((4,)),
        ],
    )(own, sent, got)
    slices = exchange(total, count, OUT_FIRST)

    tile = pl.BlockSpec((rows, LANES), lambda i: (0, i))
    whole = pl.BlockSpec((rows, state), lambda i: (0, 0))
    line = pl.BlockSpec((1, 8, rows), lambda i: (i, 0, 0))
    *scaled, near, pair_sums, db, dc = call(
        block_kernel, "block", [line, tile, tile, whole, whole],
        (*[shape(rows, height, dtype=BF16)] * 4,
         stored(rows, height), stored(pairs, 8, rows), stored(rows, state), stored(rows, state)),
        8 * square, 6 * wide, grid=(pairs,),
        out_specs=[tile] * 5 + [line, whole, whole],
        scratch_shapes=[pltpu.VMEM((rows, rows), F32)] * 2,
    )(lines, *operands)
    slices, *near_parts = lax.optimization_barrier((slices, *scaled, near, pair_sums, db, dc))
    *scaled, near, pair_sums, db, dc = near_parts
    before = call(
        functools.partial(scan_kernel, per), "scan", [SMEM, VMEM], shape(chips, per // 4, 4, state),
        height * state, wide, out_specs=VMEM,
    )(late, slices)
    back = exchange(before, count, BACK_FIRST)
    theirs = swap_cores(back, count)
    through, far = call(
        functools.partial(through_kernel, heads), "through", [SMEM] + [VMEM] * 6,
        (stored(height, state), shape(rows, state)), square, 3 * wide, out_specs=(HBM, VMEM),
        scratch_shapes=[pltpu.VMEM((height, state), F32), pltpu.SemaphoreType.DMA],
    )(late, back, got, *scaled)
    packed = call(
        rows_kernel, "rows", [SMEM] + [VMEM] * 8, stored(parts, 2 * rows // parts, state),
        square, 3 * wide, out_specs=HBM,
        scratch_shapes=[
            pltpu.VMEM((height, state), F32), pltpu.VMEM((parts, 2 * rows // parts, state), F32),
            pltpu.SemaphoreType.DMA((2,)),
        ],
    )(late, theirs, *scaled, far, db, dc)
    summed = jnp.sum(lax.all_to_all(packed, "tp", 0, 0, axis_index_groups=[listed(parts, SUM_FIRST)], tiled=True), axis=0)

    input_grad, decay_grad = call(
        last_kernel, "last", [SMEM] + [VMEM] * 9, (shape(rows, height), shape(heads, rows)),
        2 * square, 6 * wide, out_specs=(HBM, VMEM),
        scratch_shapes=[
            pltpu.VMEM((height, state), F32), pltpu.VMEM((rows, height), F32), pltpu.SemaphoreType.DMA((pairs,)),
        ],
    )(late, lines, through, theirs, *operands, near, pair_sums)
    tall = rows // parts
    return (input_grad, summed[:tall], summed[tall:], decay_grad)


def solution(mesh):
    placed = (P("ctx", "tp"), P("ctx", None), P("ctx", None), P("tp", "ctx"), P("ctx", "tp"))
    return jax.shard_map(
        per_device,
        mesh=mesh,
        in_specs=placed,
        out_specs=(P("ctx", "tp"), P(("ctx", "tp"), None), P(("ctx", "tp"), None), P("tp", "ctx")),
        check_vma=False,
    )
```

```python
import functools

import jax
import jax.numpy as jnp
from jax import lax
from jax.experimental import pallas as pl
from jax.experimental.pallas import tpu as pltpu
from jax.sharding import PartitionSpec as P

INTERPRET = False
F32 = jnp.float32
BF16 = jnp.bfloat16
CODE_UNIT = 2.0 ** (-16)
LANES = 128
MASKED = -1e30
GRANT = 12 << 20
OUT_FIRST = 20
BACK_FIRST = 20
SUM_FIRST = 3

VMEM = pl.BlockSpec(memory_space=pltpu.VMEM)
SMEM = pl.BlockSpec(memory_space=pltpu.SMEM)
HBM = pl.BlockSpec(memory_space=pltpu.HBM)


def listed(members, first):
    first = first % members
    return [first] + [k for k in reversed(range(members)) if k != first]


def split(a):
    high = a.astype(BF16)
    return high, (a - high.astype(F32)).astype(BF16)


def nn(a, b):
    return lax.dot_general(a, b, (((1,), (0,)), ((), ())), preferred_element_type=F32)


def nt(a, b):
    return lax.dot_general(a, b, (((1,), (1,)), ((), ())), preferred_element_type=F32)


def three(product, a, b):
    return product(a[0], b[0]) + (product(a[0], b[1]) + product(a[1], b[0]))


def iota(shape, axis):
    return lax.broadcasted_iota(jnp.int32, shape, axis)


def spread(columns, pair, rows):
    first = columns[:, 2 * pair : 2 * pair + 1]
    second = columns[:, 2 * pair + 1 : 2 * pair + 2]
    return jnp.where(iota((rows, LANES), 1) < LANES // 2, first, second)


def pair_state(scale, source_ref, side, pair, out_ref):
    half = LANES // 2
    turned = source_ref[:, pair * LANES : (pair + 1) * LANES].T
    first = turned[:half, :] * scale[2 * pair : 2 * pair + 1, :]
    second = turned[half:, :] * scale[2 * pair + 1 : 2 * pair + 2, :]
    scaled = jnp.concatenate([first, second], axis=0)
    out_ref[pair * LANES : (pair + 1) * LANES, :] = three(nn, split(scaled), side)


def halves(codes):
    return (codes >> 8).astype(F32).astype(BF16), (codes & 255).astype(F32).astype(BF16)


def decay_lines(codes):
    rows = codes.shape[1]
    high, low = halves(codes)
    upper = jnp.where(iota((rows, rows), 0) <= iota((rows, rows), 1), 1.0, 0.0).astype(BF16)
    return (256.0 * nn(high, upper) + nn(low, upper)) * -CODE_UNIT


def lead_kernel(
    late_ref, codes_hbm, x_hbm, dy_hbm, b_hbm, c_hbm,
    sent_ref, pairs_ref, codes_ref, x_ref, dy_ref, b_ref, c_ref, sems,
):
    pairs = x_ref.shape[1] // LANES

    def wide(source, target, slot):
        parts = [pl.ds(pair * LANES, LANES) for pair in range(pairs)]
        return [pltpu.make_async_copy(source.at[:, p], target.at[:, p], sems.at[slot + i]) for i, p in enumerate(parts)]

    fetch_codes = pltpu.make_async_copy(codes_hbm, codes_ref, sems.at[0])
    fetch_codes.start()
    fetch_x = [pltpu.make_async_copy(b_hbm, b_ref, sems.at[1]), *wide(x_hbm, x_ref, 2)]
    fetch_dy = [pltpu.make_async_copy(c_hbm, c_ref, sems.at[2 + pairs]), *wide(dy_hbm, dy_ref, 3 + pairs)]

    @pl.when(late_ref[0] == 1)
    def _():
        for copy in fetch_dy + fetch_x:
            copy.start()

    @pl.when(late_ref[0] == 0)
    def _():
        for copy in fetch_x + fetch_dy:
            copy.start()

    fetch_codes.wait()
    within = decay_lines(codes_ref[...])
    heads, rows = within.shape
    pairs_ref[...] = jnp.zeros_like(pairs_ref)
    for pair in range(pairs):
        pairs_ref[pair, 0:2, :] = within[2 * pair : 2 * pair + 2, :]
    final = within[:, rows - 1 : rows]
    decay = jnp.exp(final)
    lane = iota((8, LANES), 1)
    line = jnp.zeros((8, LANES), F32)
    for head in range(heads):
        line = jnp.where(lane == head, decay[head : head + 1, :], line)
    sent_ref[x_ref.shape[1] :, :] = line

    def run(scale, source_ref, side_ref, copies, others):
        copies[0].wait()
        side = split(side_ref[...])
        for pair in range(pairs):
            copies[1 + pair].wait()
            pair_state(scale, source_ref, side, pair, sent_ref)
        for copy in others:
            copy.wait()

    @pl.when(late_ref[0] == 1)
    def _():
        run(jnp.exp(within), dy_ref, c_ref, fetch_dy, fetch_x)

    @pl.when(late_ref[0] == 0)
    def _():
        run(jnp.exp(final - within), x_ref, b_ref, fetch_x, fetch_dy)


def own_kernel(late_ref, codes_ref, x_ref, dy_ref, b_ref, c_ref, own_ref):
    within = decay_lines(codes_ref[...])
    rows = within.shape[1]

    def run(scale, source_ref, side_ref):
        side = split(side_ref[...])
        for pair in range(source_ref.shape[1] // LANES):
            pair_state(scale, source_ref, side, pair, own_ref)

    @pl.when(late_ref[0] == 0)
    def _():
        run(jnp.exp(within), dy_ref, c_ref)

    @pl.when(late_ref[0] == 1)
    def _():
        run(jnp.exp(within[:, rows - 1 : rows] - within), x_ref, b_ref)


def chip_kernel(heads, own_ref, sent_ref, got_ref, slab_hbm, total_ref, slab_ref, sems):
    height = own_ref.shape[0]
    width = height // heads
    chips, slab, lanes = slab_ref.shape
    per = height // chips
    mine = sent_ref[height : height + 1, :]
    theirs = got_ref[height : height + 1, :]
    for head in range(heads):
        part = slice(head * width, (head + 1) * width)
        total_ref[part, :] = own_ref[part, :] + mine[:, head : head + 1] * got_ref[part, :]
    both = mine * theirs
    lane = iota((slab - per, lanes), 1)
    line = iota((slab - per, lanes), 0)
    copies = []
    batch = chips // sems.shape[0]
    for chip in range(chips):
        slab_ref[chip, 0:per, :] = total_ref[chip * per : (chip + 1) * per, :]
        extra = jnp.zeros((slab - per, lanes), F32)
        for head in range(heads):
            low = max(head * width - chip * per, 0)
            high = min((head + 1) * width - chip * per, per)
            if low < high:
                here = (lane >= low) & (lane < high) & (line == 0)
                extra = jnp.where(here, both[:, head : head + 1], extra)
        slab_ref[chip, per:slab, :] = extra
        if (chip + 1) % batch == 0:
            part = pl.ds(chip + 1 - batch, batch)
            copies.append(pltpu.make_async_copy(slab_ref.at[part], slab_hbm.at[part], sems.at[len(copies)]))
            copies[-1].start()
    for copy in copies:
        copy.wait()


def scan_kernel(per, late_ref, got_ref, out_ref):
    chips, slab, lanes = got_ref.shape
    diagonal = iota((slab, lanes), 0) == iota((slab, lanes), 1)

    arrived, leaving = listed(chips, OUT_FIRST), listed(chips, BACK_FIRST)

    def run(order):
        carried = jnp.zeros((slab, lanes), F32)
        for chip in order:
            at, to = arrived.index(chip), leaving.index(chip)
            factor = jnp.sum(jnp.where(diagonal, got_ref[at, per : per + 1, :], 0.0), axis=1, keepdims=True)
            for i in range(per // 4):
                out_ref[to, i] = carried[4 * i : 4 * i + 4, :]
            carried = factor * carried + got_ref[at]

    @pl.when(late_ref[0] == 1)
    def _():
        run(range(chips))

    @pl.when(late_ref[0] == 0)
    def _():
        run(range(chips - 1, -1, -1))


def unpack(slab_ref, out_ref):
    chips, pieces, tall, _ = slab_ref.shape
    owned = listed(chips, OUT_FIRST)
    for place, chip in enumerate(listed(chips, BACK_FIRST)):
        for i in range(pieces):
            at = (owned.index(chip) * pieces + i) * tall
            out_ref[at : at + tall, :] = slab_ref[place, i]


def block_kernel(
    pairs_ref, x_ref, dy_ref, b_ref, c_ref,
    xs_high, xs_low, dys_high, dys_low, dx_ref, pair_ref, db_ref, dc_ref,
    scores_ref, grads_ref,
):
    step = pl.program_id(0)
    rows = x_ref.shape[0]
    half = rows // 2

    @pl.when(step == 0)
    def _():
        scores_ref[...] = three(nt, split(b_ref[...]), split(c_ref[...]))
        grads_ref[...] = jnp.zeros_like(grads_ref)

    lines = pairs_ref[0]
    columns = lines.T
    x = x_ref[...]
    dy = dy_ref[...]
    xs = split(x * spread(jnp.exp(lines.T[rows - 1 : rows, :] - columns), 0, rows))
    dys = split(dy * spread(jnp.exp(columns), 0, rows))
    xs_high[...], xs_low[...] = xs
    dys_high[...], dys_low[...] = dys
    x_high, x_low = split(x)
    left = iota((rows, LANES), 1) < LANES // 2
    lane = iota((rows, LANES), 1)
    sent = jnp.zeros((rows, LANES), F32)
    received = []
    totals = [0.0, 0.0]
    for i in range(2):
        masked = split(jnp.where(left if i == 0 else ~left, dy, 0.0))
        source_sums = []
        target_sum = None
        for b, start in enumerate((0, half)):
            part = slice(start, start + half)
            target = tuple(m[start:, :] for m in masked)
            products = three(nt, (x_high[part], x_low[part]), target)
            gap = lines[i : i + 1, start:] - columns[part, i : i + 1]
            shape = (half, rows - start)
            decays = jnp.exp(jnp.where(iota(shape, 1) >= iota(shape, 0), gap, MASKED))
            scores = scores_ref[part, start:]
            weighted = decays * products
            grads_ref[part, start:] += weighted
            terms = weighted * scores
            source_sums.append(jnp.sum(terms, axis=1, keepdims=True))
            sums = jnp.sum(terms, axis=0, keepdims=True)
            if b == 0:
                target_sum = sums
            else:
                target_sum = jnp.concatenate([target_sum[:, :half], target_sum[:, half:] + sums], axis=1)
            totals[b] += three(nn, split(decays * scores), target)
        sent = jnp.where(lane == i, jnp.concatenate(source_sums, axis=0), sent)
        received.append(target_sum)
    dx_ref[0:half, :] = totals[0]
    dx_ref[half:, :] = totals[1]
    line = iota((8, rows), 0)
    gained = jnp.where(line == 0, received[0], jnp.where(line == 1, received[1], 0.0))
    pair_ref[0] = gained - sent.T[0:8, :]

    @pl.when(step == pl.num_programs(0) - 1)
    def _():
        grads = grads_ref[...]
        db_ref[...] = three(nn, split(grads), split(c_ref[...]))
        dc_ref[...] = three(nn, split(grads.T), split(b_ref[...]))


def through_kernel(
    heads, late_ref, back_ref, got_ref, xs_high, xs_low, dys_high, dys_low, through_hbm, far_ref, through_ref, sem
):
    height = through_ref.shape[0]
    width = height // heads
    unpack(back_ref, through_ref)
    decay = got_ref[height : height + 1, :]
    for head in range(heads):
        part = slice(head * width, (head + 1) * width)
        through_ref[part, :] = decay[:, head : head + 1] * through_ref[part, :] + got_ref[part, :]
    copy = pltpu.make_async_copy(through_ref, through_hbm, sem)
    copy.start()

    @pl.when(late_ref[0] == 1)
    def _():
        far_ref[...] = three(nn, (dys_high[...], dys_low[...]), split(through_ref[...]))

    @pl.when(late_ref[0] == 0)
    def _():
        far_ref[...] = three(nn, (xs_high[...], xs_low[...]), split(through_ref[...]))

    copy.wait()


def rows_kernel(
    late_ref, theirs_ref, xs_high, xs_low, dys_high, dys_low, far_ref, db_ref, dc_ref, out_hbm, state_ref, out_ref, sems
):
    unpack(theirs_ref, state_ref)
    parts, tall, _ = out_ref.shape
    tall = tall // 2
    places = listed(parts, SUM_FIRST)

    def send(which, value):
        side = slice(which * tall, (which + 1) * tall)
        for part in range(parts):
            out_ref[places.index(part), side, :] = value[part * tall : (part + 1) * tall, :]
        copy = pltpu.make_async_copy(
            out_ref.at[:, pl.ds(which * tall, tall), :], out_hbm.at[:, pl.ds(which * tall, tall), :], sems.at[which]
        )
        copy.start()
        return copy

    @pl.when(late_ref[0] == 1)
    def _():
        first = send(1, dc_ref[...] + far_ref[...])
        second = send(0, db_ref[...] + three(nn, (xs_high[...], xs_low[...]), split(state_ref[...])))
        first.wait()
        second.wait()

    @pl.when(late_ref[0] == 0)
    def _():
        first = send(0, db_ref[...] + far_ref[...])
        second = send(1, dc_ref[...] + three(nn, (dys_high[...], dys_low[...]), split(state_ref[...])))
        first.wait()
        second.wait()


def last_kernel(
    late_ref, pairs_ref, through_ref, slab_ref, x_ref, dy_ref, b_ref, c_ref, near_ref, pair_ref,
    dx_hbm, out_ref, theirs_ref, dx_ref, sems,
):
    rows, height = x_ref.shape
    pairs = height // LANES
    half = LANES // 2
    late = late_ref[0] == 1
    unpack(slab_ref, theirs_ref)
    b, c = split(b_ref[...]), split(c_ref[...])
    picks = jnp.where((iota((8, LANES), 1) < half) == (iota((8, LANES), 0) == 0), 1.0, 0.0)
    picks = jnp.where(iota((8, LANES), 0) < 2, picks, 0.0).astype(BF16)
    first, second = iota((rows, rows), 0), iota((rows, rows), 1)
    earlier = jnp.where(first < second, 1.0, 0.0).astype(BF16)
    line = iota((8, rows), 0)
    copies = []
    left_lines, through_lines, enter_lines = [], [], []
    for pair in range(pairs):
        part = slice(pair * LANES, (pair + 1) * LANES)
        lines = pairs_ref[pair]
        columns = lines.T
        mine, other = through_ref[part, :], theirs_ref[part, :]
        start = jnp.where(late, mine, other)
        end = jnp.where(late, other, mine)
        entered = three(nt, c, split(start)) * spread(jnp.exp(columns), 0, rows)
        leaving = three(nt, b, split(end)) * spread(jnp.exp(columns[rows - 1 : rows, :] - columns), 0, rows)
        dx_ref[:, part] = near_ref[:, part] + leaving
        copies.append(pltpu.make_async_copy(dx_ref.at[:, part], dx_hbm.at[:, part], sems.at[pair]))
        copies[-1].start()
        enter = split(dy_ref[:, part] * entered)
        leave = split(x_ref[:, part] * leaving)
        enter_lines.append(nt(picks, enter[0]) + nt(picks, enter[1]))
        left_lines.append(nt(picks, leave[0]) + nt(picks, leave[1]))
        across = jnp.sum(mine * other, axis=1, keepdims=True)
        passed = [jnp.sum(across[i * half : (i + 1) * half], axis=0, keepdims=True) for i in range(2)]
        decay = jnp.exp(lines[:, rows - 1 : rows])
        through_lines.append(decay * jnp.where(line == 0, passed[0], jnp.where(line == 1, passed[1], 0.0)))
    later = jnp.where(first >= second, 1.0, 0.0).astype(BF16)

    def exact(lines, ones):
        a = jnp.concatenate(lines, axis=0)
        high, low = split(a)
        rest = (a - high.astype(F32) - low.astype(F32)).astype(BF16)
        return nn(high, ones) + (nn(low, ones) + nn(rest, ones))

    gained = exact([pair_ref[p] + enter_lines[p] for p in range(pairs)], later) + exact(left_lines, earlier)
    total = gained + jnp.concatenate(through_lines, axis=0)
    for pair in range(pairs):
        out_ref[2 * pair : 2 * pair + 2, :] = total[8 * pair : 8 * pair + 2, :]
    for copy in copies:
        copy.wait()


def call(kernel, name, in_specs, out_shape, flops, moved, grant=GRANT, **rest):
    return pl.pallas_call(
        kernel,
        name=name,
        in_specs=in_specs,
        out_shape=out_shape,
        cost_estimate=pl.CostEstimate(flops=flops, bytes_accessed=moved, transcendentals=0),
        interpret=INTERPRET,
        compiler_params=pltpu.CompilerParams(vmem_limit_bytes=grant),
        **rest,
    )


def shape(*dims, dtype=F32):
    return jax.ShapeDtypeStruct(dims, dtype)


def stored(*dims):
    return shape(*dims) if INTERPRET else pltpu.HBM(dims, F32)


def swap_cores(value, count):
    return lax.ppermute(value, "ctx", [(i, i ^ 1) for i in range(count)])


def exchange(value, count, first):
    groups = [[2 * k + c for k in listed(count // 2, first)] for c in range(2)]
    return lax.all_to_all(value, "ctx", 0, 0, axis_index_groups=groups, tiled=True)


def per_device(inputs, state_input, state_output, decay_codes, output_grad):
    count = lax.axis_size("ctx")
    parts = lax.axis_size("tp")
    heads, rows = decay_codes.shape
    height = inputs.shape[1]
    state = state_input.shape[1]
    pairs = height // LANES
    chips = count // 2
    per = height // chips
    slab = -(-(per + 1) // 8) * 8
    late = (lax.axis_index("ctx") & 1).astype(jnp.int32).reshape(1)
    operands = (inputs, output_grad, state_input, state_output)
    wide = rows * height * 4
    square = 2 * rows * height * state * 3

    given = (decay_codes, *operands)
    sent, lines, codes, *operands = call(
        lead_kernel, "lead", [SMEM] + [HBM] * 5,
        (shape(height + 8, state), shape(pairs, 8, rows), *[shape(*a.shape, dtype=a.dtype) for a in given]),
        square, 2 * wide, out_specs=(VMEM,) * 7, scratch_shapes=[pltpu.SemaphoreType.DMA((3 + 2 * pairs,))],
    )(late, *[a if INTERPRET else pltpu.with_memory_space_constraint(a, pltpu.HBM) for a in given])
    got = swap_cores(sent, count)
    own = call(
        own_kernel, "own", [SMEM] + [VMEM] * 5, shape(height, state), square, 3 * wide, out_specs=VMEM,
    )(late, codes, *operands)
    total = call(
        functools.partial(chip_kernel, heads), "chip", [VMEM] * 3, stored(chips, slab, state),
        height * state, wide, out_specs=HBM,
        scratch_shapes=[
            pltpu.VMEM((height, state), F32), pltpu.VMEM((chips, slab, state), F32), pltpu.SemaphoreType.DMA((4,)),
        ],
    )(own, sent, got)
    slices = exchange(total, count, OUT_FIRST)

    tile = pl.BlockSpec((rows, LANES), lambda i: (0, i))
    whole = pl.BlockSpec((rows, state), lambda i: (0, 0))
    line = pl.BlockSpec((1, 8, rows), lambda i: (i, 0, 0))
    *scaled, near, pair_sums, db, dc = call(
        block_kernel, "block", [line, tile, tile, whole, whole],
        (*[shape(rows, height, dtype=BF16)] * 4,
         stored(rows, height), stored(pairs, 8, rows), stored(rows, state), stored(rows, state)),
        8 * square, 6 * wide, grid=(pairs,),
        out_specs=[tile] * 5 + [line, whole, whole],
        scratch_shapes=[pltpu.VMEM((rows, rows), F32)] * 2,
    )(lines, *operands)
    slices, *near_parts = lax.optimization_barrier((slices, *scaled, near, pair_sums, db, dc))
    *scaled, near, pair_sums, db, dc = near_parts
    before = call(
        functools.partial(scan_kernel, per), "scan", [SMEM, VMEM], shape(chips, per // 4, 4, state),
        height * state, wide, out_specs=VMEM,
    )(late, slices)
    back = exchange(before, count, BACK_FIRST)
    theirs = swap_cores(back, count)
    through, far = call(
        functools.partial(through_kernel, heads), "through", [SMEM] + [VMEM] * 6,
        (stored(height, state), shape(rows, state)), square, 3 * wide, out_specs=(HBM, VMEM),
        scratch_shapes=[pltpu.VMEM((height, state), F32), pltpu.SemaphoreType.DMA],
    )(late, back, got, *scaled)
    packed = call(
        rows_kernel, "rows", [SMEM] + [VMEM] * 8, stored(parts, 2 * rows // parts, state),
        square, 3 * wide, out_specs=HBM,
        scratch_shapes=[
            pltpu.VMEM((height, state), F32), pltpu.VMEM((parts, 2 * rows // parts, state), F32),
            pltpu.SemaphoreType.DMA((2,)),
        ],
    )(late, theirs, *scaled, far, db, dc)
    summed = jnp.sum(lax.all_to_all(packed, "tp", 0, 0, axis_index_groups=[listed(parts, SUM_FIRST)], tiled=True), axis=0)

    input_grad, decay_grad = call(
        last_kernel, "last", [SMEM] + [VMEM] * 9, (shape(rows, height), shape(heads, rows)),
        2 * square, 6 * wide, out_specs=(HBM, VMEM),
        scratch_shapes=[
            pltpu.VMEM((height, state), F32), pltpu.VMEM((rows, height), F32), pltpu.SemaphoreType.DMA((pairs,)),
        ],
    )(late, lines, through, theirs, *operands, near, pair_sums)
    tall = rows // parts
    return (input_grad, summed[:tall], summed[tall:], decay_grad)


def solution(mesh):
    placed = (P("ctx", "tp"), P("ctx", None), P("ctx", None), P("tp", "ctx"), P("ctx", "tp"))
    return jax.shard_map(
        per_device,
        mesh=mesh,
        in_specs=placed,
        out_specs=(P("ctx", "tp"), P(("ctx", "tp"), None), P(("ctx", "tp"), None), P("tp", "ctx")),
        check_vma=False,
    )
```
